256 devices in a mesh: gx: 4 (over x), gy: 4 (over y), gz: 16 (over z, core).
Axes of the slice: x: 4, y: 4, z: 8, core: 2. Of those that a mesh axis runs over, the one named last changes fastest.
Arguments:
- solution: float32 [3, 32, 32, 4096], P(None, 'gx', 'gy', 'gz'), may hold values from -6 to 6
- residual: float32 [3, 32, 32, 4096], P(None, 'gx', 'gy', 'gz'), may hold values from -6 to 6
- prev_direction: float32 [3, 32, 32, 4096], P(None, 'gx', 'gy', 'gz'), may hold values from -6 to 6
- prev_image: float32 [3, 32, 32, 4096], P(None, 'gx', 'gy', 'gz'), may hold values from -6 to 6
- prev_rz: float32 [], replicated, may hold values from 4194304 to 16777216
- density_index: int32 [32, 32, 4096], P('gx', 'gy', 'gz'), may hold values from 0 to 15
- stiffness_table: float32 [16], replicated, may hold values from 0.2 to 2
- coarse_inverse: float32 [4, 4, 384, 384], P('gx', 'gy'), may hold values from -0.05 to 5, as said below
Outputs:
- new_solution: float32 [3, 32, 32, 4096], P(None, 'gx', 'gy', 'gz')
- new_residual: float32 [3, 32, 32, 4096], P(None, 'gx', 'gy', 'gz')
- direction: float32 [3, 32, 32, 4096], P(None, 'gx', 'gy', 'gz')
- image: float32 [3, 32, 32, 4096], P(None, 'gx', 'gy', 'gz')
The draws below stay inside these ranges and needn't reach their ends.
Inputs may be any that keep to these rules, and one draw needn't show every extreme that they name: `coarse_inverse`: each group's matrix is symmetric positive definite.
All inputs are finite; a program needn't handle non-finite values.
Results may differ from the reference program's by a relative error of at most 0.00016.
Values sent between devices are 32-bit elements; how exact they have to be, the bound alone decides.
A program may use at most 128 MiB of HBM per device.

```python
import math
import jax
import jax.numpy as jnp
from jax import lax

CX = 8
CY = 8
CZ = 256
LEVELS = 16
SWEEPS = 2
NX = 32
NY = 32
NZ = 4096
KC = 384
N_GX = 4
N_GY = 4
N_GZ = 16


def draw_coarse_inverse(key, part):
    key_off = jax.random.fold_in(key, 11)
    key_diag = jax.random.fold_in(key, 12)
    spread = 0.5 / KC
    raw = jax.random.uniform(key_off, (N_GX, N_GY, KC, KC), jnp.float32, -0.5 * spread, 0.5 * spread)
    symmetric = raw + jnp.swapaxes(raw, 2, 3)
    identity = jnp.eye(KC, dtype=jnp.float32)
    index = jnp.arange(KC, dtype=jnp.int32)
    group = index // 24
    component = index % 24 // 8
    place_x = (index % 8 // 4).astype(jnp.float32)
    place_y = (index % 4 // 2).astype(jnp.float32)
    place_z = (2 * group + index % 2).astype(jnp.float32)
    delta_x = place_x[:, None] - place_x[None, :]
    delta_y = place_y[:, None] - place_y[None, :]
    delta_z = place_z[:, None] - place_z[None, :]
    distance = jnp.sqrt(delta_x * delta_x + delta_y * delta_y + delta_z * delta_z)
    coupling = jnp.where(component[:, None] == component[None, :], 1.0, 0.3).astype(jnp.float32)
    kernel = 0.12 * coupling * jnp.exp(-distance / 4.0)
    diag_values = jax.random.uniform(key_diag, (N_GX, N_GY, KC), jnp.float32, 1.0, 2.0)
    matrix = symmetric * (1.0 - identity) + diag_values[:, :, :, None] * identity + kernel[None, None, :, :]
    return matrix


def plant(drawn, rng, least, top_value):
    longest = drawn.shape.index(max(drawn.shape))
    spots = []
    for shift in (0, 1):
        where = [jax.random.randint(jax.random.fold_in(rng, axis), (), 0, length) for axis, length in enumerate(drawn.shape)]
        where[longest] = (where[longest] + shift) % drawn.shape[longest]
        spots.append(tuple(where))
    return drawn.at[spots[0]].set(least).at[spots[1]].set(top_value)


def level_of(key, dims, pieces, least, largest):
    factor_of, own = 1.0, jax.random.fold_in(key, 6)
    for position, blocks in pieces:
        steps = jnp.exp(jax.random.uniform(jax.random.fold_in(own, position), (blocks,), jnp.float32, least / len(pieces), largest / len(pieces)))
        factor_of = factor_of * jnp.repeat(steps, dims[position] // blocks).reshape([-1 if axis == position else 1 for axis in range(len(dims))])
    return factor_of


def bell_draw(own_key, shape, deviation, bound, pieces=(), kind=jnp.bfloat16):
    factor_of = level_of(own_key, shape, pieces, -0.22, 0.18) if pieces else 1.0
    entries = jax.random.normal(own_key, shape, jnp.float32) * deviation * factor_of
    return jnp.minimum(jnp.maximum(entries, -bound), bound).astype(kind)


def setup_inputs(seed: int = 0) -> dict:
    key_list = jax.random.split(jax.random.key(seed), 9)
    solution = bell_draw(key_list[0], (3, NX, NY, NZ), 1.0, 6.0, ((1, 4), (2, 4), (3, 16)), jnp.float32)
    residual = bell_draw(key_list[1], (3, NX, NY, NZ), 1.0, 6.0, ((1, 4), (2, 4), (3, 16)), jnp.float32)
    prev_direction = bell_draw(key_list[2], (3, NX, NY, NZ), 1.0, 6.0, ((1, 4), (2, 4), (3, 16)), jnp.float32)
    prev_image = bell_draw(key_list[3], (3, NX, NY, NZ), 1.0, 6.0, ((1, 4), (2, 4), (3, 16)), jnp.float32)
    prev_rz = jnp.clip(jnp.exp(jax.random.uniform(key_list[4], (), jnp.float32, math.log(4194304), math.log(16777216))), 4194304, 16777216)
    density_index = plant(jax.random.randint(key_list[5], (NX, NY, NZ), 0, LEVELS), jax.random.fold_in(key_list[5], 1), 0, LEVELS - 1).astype(jnp.int32)
    stiffness_table = jnp.clip(jnp.exp(jax.random.uniform(key_list[6], (LEVELS,), jnp.float32, math.log(0.2), math.log(2.0))), 0.2, 2.0)
    coarse_inverse = draw_coarse_inverse(jax.random.fold_in(key_list[8], 71), 0)
    return dict(solution=solution, residual=residual, prev_direction=prev_direction, prev_image=prev_image, prev_rz=prev_rz, density_index=density_index, stiffness_table=stiffness_table, coarse_inverse=coarse_inverse)


COUPLING = ((1.0, 0.3, 0.3), (0.3, 1.0, 0.3), (0.3, 0.3, 1.0))
DAMPING = 0.6
MASS_SHIFT = 0.1
WEIGHT_BY_KIND = (0.0, 0.1, 0.05, 0.025)

def neighbour_list():
    listing = []
    for step_x in (-1, 0, 1):
        for step_y in (-1, 0, 1):
            for step_z in (-1, 0, 1):
                kind = abs(step_x) + abs(step_y) + abs(step_z)
                if kind > 0:
                    listing.append((step_x, step_y, step_z, 0.5 * WEIGHT_BY_KIND[kind]))
    return listing

def stencil(padded, coeff):
    size_x = padded.shape[1] - 2
    size_y = padded.shape[2] - 2
    size_z = padded.shape[3] - 2
    centre = padded[:, 1:-1, 1:-1, 1:-1]
    coeff_centre = coeff[1:-1, 1:-1, 1:-1]
    total = MASS_SHIFT * coeff_centre * centre
    for step_x, step_y, step_z, weight in neighbour_list():
        other = padded[:, 1 + step_x:1 + step_x + size_x, 1 + step_y:1 + step_y + size_y, 1 + step_z:1 + step_z + size_z]
        other_coeff = coeff[1 + step_x:1 + step_x + size_x, 1 + step_y:1 + step_y + size_y, 1 + step_z:1 + step_z + size_z]
        total = total + weight * (coeff_centre + other_coeff) * (centre - other)
    return jnp.stack([COUPLING[line][0] * total[0] + COUPLING[line][1] * total[1] + COUPLING[line][2] * total[2] for line in range(3)])

def diagonal_of(coeff):
    size_x = coeff.shape[0] - 2
    size_y = coeff.shape[1] - 2
    size_z = coeff.shape[2] - 2
    coeff_centre = coeff[1:-1, 1:-1, 1:-1]
    total = MASS_SHIFT * coeff_centre
    for step_x, step_y, step_z, weight in neighbour_list():
        other_coeff = coeff[1 + step_x:1 + step_x + size_x, 1 + step_y:1 + step_y + size_y, 1 + step_z:1 + step_z + size_z]
        total = total + weight * (coeff_centre + other_coeff)
    return total

def pad_field(field):
    return jnp.pad(field, ((0, 0), (1, 1), (1, 1), (1, 1)))

def boxed_sum(field, box_x, box_y, box_z):
    shaped = field.reshape(3, field.shape[1] // box_x, box_x, field.shape[2] // box_y, box_y, field.shape[3] // box_z, box_z)
    return lax.optimization_barrier(jnp.sum(shaped, axis=(2, 4, 6)))

def coarsen_cells(cells):
    shaped = cells.reshape(cells.shape[0] // 2, 2, cells.shape[1] // 2, 2, cells.shape[2] // 2, 2)
    return lax.optimization_barrier(jnp.sum(shaped, axis=(1, 3, 5))) * 0.125

def spread_up(field, box_x, box_y, box_z):
    comps, size_x, size_y, size_z = field.shape
    wide = jnp.broadcast_to(field[:, :, None, :, None, :, None], (comps, size_x, box_x, size_y, box_y, size_z, box_z))
    return wide.reshape(comps, size_x * box_x, size_y * box_y, size_z * box_z)

def reference(solution, residual, prev_direction, prev_image, prev_rz, density_index, stiffness_table, coarse_inverse):
    young = stiffness_table[density_index]
    coeff_fine = jnp.pad(young, 1)
    diag_fine = diagonal_of(coeff_fine)

    def fine_apply(field):
        return stencil(pad_field(field), coeff_fine)
    smooth = DAMPING * residual / diag_fine
    for sweep_index in range(SWEEPS - 1):
        smooth = smooth + DAMPING * (residual - fine_apply(smooth)) / diag_fine
    rest = residual - fine_apply(smooth)
    coarse_rhs = 0.5 * boxed_sum(rest, 2, 2, 2)
    coeff_mid = jnp.pad(coarsen_cells(young), 1)
    diag_mid = diagonal_of(coeff_mid)
    middle = DAMPING * coarse_rhs / diag_mid
    mid_rest = coarse_rhs - stencil(pad_field(middle), coeff_mid)
    box_x = CX // 4
    box_y = CY // 4
    box_z = CZ // 4
    lowest = boxed_sum(mid_rest, box_x, box_y, box_z) * (1.0 / math.sqrt(box_x * box_y * box_z))
    gathered = lowest.reshape(3, N_GX, 2, N_GY, 2, N_GZ, 2).transpose(1, 3, 5, 0, 2, 4, 6).reshape(N_GX, N_GY, KC)
    solved = jnp.einsum('abij,abj->abi', coarse_inverse, gathered, precision=lax.Precision.HIGHEST)
    correction = solved.reshape(N_GX, N_GY, N_GZ, 3, 2, 2, 2).transpose(3, 0, 4, 1, 5, 2, 6).reshape(3, 2 * N_GX, 2 * N_GY, 2 * N_GZ)
    middle = middle + spread_up(correction, box_x, box_y, box_z)
    middle = middle + DAMPING * (coarse_rhs - stencil(pad_field(middle), coeff_mid)) / diag_mid
    smooth = smooth + spread_up(middle, 2, 2, 2)
    for sweep_index in range(SWEEPS):
        smooth = smooth + DAMPING * (residual - fine_apply(smooth)) / diag_fine
    precond = smooth
    inner_rz = jnp.sum(residual * precond)
    beta = inner_rz / prev_rz
    direction = precond + beta * prev_direction
    image = fine_apply(precond) + beta * prev_image
    alpha = inner_rz / jnp.sum(direction * image)
    new_solution = solution + alpha * direction
    new_residual = residual - alpha * image
    return (new_solution, new_residual, direction, image)
```

```python
import functools
import itertools
import math

import jax
import jax.numpy as jnp
from jax import lax
from jax.experimental import pallas as pl
from jax.experimental.pallas import tpu as pltpu
from jax.sharding import PartitionSpec as P


MESH = pl.DeviceIdType.MESH
AXES = ("gx", "gy", "gz")
F32 = jnp.float32
HIGH = lax.Precision.HIGHEST
DAMP = 0.6
EIGHTIETH = 0.0125
SMALL = (-1, 0, 1)


def iota(shape, dim):
    return lax.broadcasted_iota(jnp.int32, shape, dim)


def smooth_rows_lanes(v):
    rows, lanes = v.shape
    v = (v + v) + (pltpu.roll(v, 1, 0) + pltpu.roll(v, rows - 1, 0))
    return (v + v) + (pltpu.roll(v, 1, 1) + pltpu.roll(v, lanes - 1, 1))


def three(low, mid, high):
    return (mid + mid) + (low + high)


def operate(field, coeff, centre, at):
    e_low, e_mid, e_high = coeff(at - 1), coeff(at), coeff(at + 1)
    own = centre(at)
    parts = []
    for c in range(3):
        low, mid, high = field(c, at - 1), field(c, at), field(c, at + 1)
        plain = smooth_rows_lanes(three(low, mid, high))
        scaled = smooth_rows_lanes(three(e_low * low, e_mid * mid, e_high * high))
        parts.append(own * mid - EIGHTIETH * (e_mid * plain + scaled))
    shared = 0.3 * (parts[0] + parts[1] + parts[2])
    return [0.7 * part + shared for part in parts]


def centre_terms(low, mid, high):
    wide = EIGHTIETH * smooth_rows_lanes(three(low, mid, high))
    inverse = jnp.where(mid > 0.0, DAMP / (0.7 * mid + wide), 0.0)
    return 0.9 * mid + wide, inverse


def dot(a, b):
    return jnp.dot(a, b, precision=HIGH, preferred_element_type=F32)


def kernel(
    ng,
    res_hbm, dir_hbm, img_hbm, dens_hbm, inv_hbm, table, prev_rz,
    p_out, ap_out, ab_out,
    dens, res, ewide, emask, e16, cen, dinv, s_a, s_b, pdir, pimg,
    spack, srecv, ysum, km, cen1, dinv1, m_a, tlow,
    mpack, mrecv, wd, cenw, dinvw, m_b, m_c, u8,
    rz_mat, gsend, grecv, rows, vown, vrecv,
    dsend, drecv, esend, erecv,
    lsem, sems, recs,
):
    gx, gy, gz = (lax.axis_index(a) for a in AXES)
    me = (gx, gy, gz)

    def device(d):
        return tuple(lax.rem(me[i] + (d[i] % ng[i]), ng[i]) for i in range(3))

    near = [d for d in itertools.product(SMALL, repeat=3) if d != (0, 0, 0)]
    flat = [d for d in near if d[2] == 0]
    column = [(0, 0, k) for k in range(1, ng[2])]
    layer = [(i, j, 0) for i in range(ng[0]) for j in range(ng[1]) if (i, j) != (0, 0)]
    partners = []
    for d in near + column + layer:
        d = tuple(d[i] % ng[i] for i in range(3))
        if d not in partners:
            partners.append(d)

    barrier = pltpu.get_barrier_semaphore()
    for d in partners:
        pl.semaphore_signal(barrier, inc=1, device_id=device(d), device_id_type=MESH)
    loads = [
        pltpu.make_async_copy(dens_hbm, dens, lsem.at[0]),
        pltpu.make_async_copy(res_hbm, res.at[:, 4:12, 0:8, 0:256], lsem.at[1]),
        pltpu.make_async_copy(dir_hbm, pdir, lsem.at[2]),
        pltpu.make_async_copy(img_hbm, pimg, lsem.at[3]),
    ]
    for b in range(3):
        block = jnp.clip(gz + (b - 1), 0, ng[2] - 1)
        start = pl.multiple_of(block * 24, 8)
        loads.append(
            pltpu.make_async_copy(
                inv_hbm.at[0, 0, pl.ds(start, 24), :], rows.at[24 * b : 24 * b + 24, :], lsem.at[4 + b]
            )
        )
    for copy in loads:
        copy.start()
    rows[72:128, :] = jnp.zeros((56, rows.shape[1]), F32)
    loads[0].wait()

    @pl.loop(0, 8)
    def _(x):
        index = dens[x]
        young = jnp.full(index.shape, table[0], F32)
        for level in range(1, table.shape[0]):
            young = jnp.where(index == level, table[level], young)
        ewide[5 + x, 8:16, 0:256] = young

    loads[1].wait()

    lane8 = iota((8, 128), 1)
    row8 = iota((8, 128), 0)
    slot8 = lane8 // 8

    def fine_tile(f, x, at):
        if f < 3:
            return res[f, 4 + x, 0:8, at : at + 128]
        return ewide[5 + x, 8:16, at : at + 128]

    for side, (at, extra) in enumerate(((0, 0), (128, 8))):
        for t in range(2):
            def pack_one(x, total, t=t, at=at, extra=extra):
                for k in range(2):
                    s = k * 8 + x
                    moved = pltpu.roll(fine_tile(2 * t + k, x, at), lax.rem(8 * s + extra, 128), 1)
                    total = jnp.where(slot8 == s, moved, total)
                return total

            spack[side, t] = lax.fori_loop(0, 8, pack_one, jnp.zeros((8, 128), F32))

    pl.semaphore_wait(barrier, len(partners))

    started = []
    counter = [0]

    def send(src, dst, d):
        k = counter[0]
        counter[0] = k + 1
        copy = pltpu.make_async_remote_copy(
            src_ref=src, dst_ref=dst, send_sem=sems.at[k], recv_sem=recs.at[k],
            device_id=device(d), device_id_type=MESH,
        )
        copy.start()
        started.append(copy)
        return copy

    round_a = []
    pick = {
        -1: (slice(4, 8), slice(12, 16)), 0: (slice(4, 12), slice(4, 12)), 1: (slice(8, 12), slice(0, 4)),
    }
    pick_row = {-1: (slice(0, 4), slice(8, 12)), 0: (slice(0, 8), slice(0, 8)), 1: (slice(4, 8), slice(12, 16))}
    pick_e = {
        -1: (slice(5, 10), slice(13, 18)), 0: (slice(5, 13), slice(5, 13)), 1: (slice(8, 13), slice(0, 5)),
    }
    pick_e_row = {-1: slice(16, 24), 0: slice(8, 16), 1: slice(0, 8)}
    main = slice(0, 256)
    for d in flat:
        src = res.at[:, pick[d[0]][0], pick_row[d[1]][0], main]
        dst = res.at[:, pick[d[0]][1], pick_row[d[1]][1], main]
        round_a.append(send(src, dst, d))
    for d in flat:
        src = ewide.at[pick_e[d[0]][0], slice(8, 16), main]
        dst = ewide.at[pick_e[d[0]][1], pick_e_row[d[1]], main]
        round_a.append(send(src, dst, d))
    for d in near:
        if d[2] != 0:
            side = 0 if d[2] < 0 else 1
            round_a.append(send(spack.at[side], srecv.at[side, 1 - d[0], 1 - d[1]], d))

    lane_of = iota((384, 256), 0)
    target = jnp.where(lane_of < 320, lane_of // 2, lane_of // 2 + 64)
    rz_mat[...] = jnp.where(iota((384, 256), 1) == target, 1.0, 0.0)

    for copy in round_a:
        copy.wait_recv()

    def rim(right, left, s):
        to_right = pltpu.roll(right, lax.rem(256 - 8 * s, 128), 1)
        to_left = pltpu.roll(left, lax.rem(256 - 8 * s - 8, 128), 1)
        return jnp.where(lane8 < 64, to_right, to_left)

    rim_lanes = slice(256, 384)
    for ox, first, count, base in ((-1, 4, 4, 0), (0, 0, 8, 4), (1, 0, 4, 12)):
        for t in range(2):
            tiles = []
            for side in range(2):
                tiles.append(srecv[side, ox + 1, 1, t] if True else None)
            mixed = [
                jnp.where(row8 < 4, srecv[side, ox + 1, 2, t], srecv[side, ox + 1, 0, t]) for side in range(2)
            ]

            @pl.loop(0, count)
            def _(i, t=t, first=first, base=base, tiles=tiles, mixed=mixed):
                for k in range(2):
                    if 2 * t + k < 3:
                        s = k * 8 + first + i
                        res[2 * t + k, base + i, 0:8, rim_lanes] = rim(tiles[0], tiles[1], s)
                        res[2 * t + k, base + i, 8:16, rim_lanes] = rim(mixed[0], mixed[1], s)

    for ox, first, count, base in ((-1, 3, 5, 0), (0, 0, 8, 5), (1, 0, 5, 13)):
        tiles = [[srecv[side, ox + 1, oy, 1] for side in range(2)] for oy in range(3)]

        @pl.loop(0, count)
        def _(i, first=first, base=base, tiles=tiles):
            for oy in range(3):
                ewide[base + i, 8 * oy : 8 * oy + 8, rim_lanes] = rim(tiles[oy][0], tiles[oy][1], 8 + first + i)

    row24 = iota((24, 384), 0)
    lane24 = iota((24, 384), 1)
    y_at = gy * 8 + row24 - 8
    z_at = gz * 256 + jnp.where(lane24 < 320, lane24, lane24 - 384)
    inside = (y_at >= 0) & (y_at < 8 * ng[1]) & (z_at >= 0) & (z_at < 256 * ng[2])
    inside = jnp.where(inside & ((lane24 < 264) | (lane24 >= 376)), 1, 0)

    @pl.loop(0, 18)
    def _(x):
        x_at = gx * 8 + x - 5
        x_in = jnp.where((x_at >= 0) & (x_at < 8 * ng[0]), 1, 0)
        emask[x] = jnp.where(inside * x_in > 0, ewide[x], 0.0)

    upper = iota((8, 384), 0) < 4

    @pl.loop(0, 16)
    def _(x):
        mid = emask[x + 1]
        own, inverse = centre_terms(emask[x], mid, emask[x + 2])
        for value, out in ((mid, e16), (own, cen), (inverse, dinv)):
            out[x, 0:8, :] = value[8:16]
            out[x, 8:16, :] = jnp.where(upper, value[16:24], value[0:8])
        for c in range(3):
            s_a[c, x] = dinv[x] * res[c, x]

    def fine(ref):
        return functools.partial(
            operate, lambda c, x: ref[c, x], lambda x: e16[x], lambda x: cen[x]
        )

    def sweep(source, out, start, stop):
        @pl.loop(start, stop)
        def _(x):
            image = fine(source)(x)
            for c in range(3):
                out[c, x] = source[c, x] + dinv[x] * (res[c, x] - image[c])

    sweep(s_a, s_b, 1, 15)

    def put_tiles(ref, f, k, value):
        for t in range(3):
            ref[f, k, t] = value[:, 128 * t : 128 * t + 128]

    @pl.loop(0, 6)
    def _(k):
        x = 2 * k + 2
        first, second = fine(s_b)(x), fine(s_b)(x + 1)
        for c in range(3):
            both = (res[c, x] - first[c]) + (res[c, x + 1] - second[c])
            put_tiles(ysum, c, k + 1, both + pltpu.roll(both, 15, 0))

    @pl.loop(0, 8)
    def _(k):
        both = e16[2 * k] + e16[2 * k + 1]
        put_tiles(ysum, 3, k, both + pltpu.roll(both, 15, 0))

    for c in range(3):
        for k in (0, 7):
            ysum[c, k] = jnp.zeros((3, 16, 128), F32)

    total = None
    for t in range(3):
        left = ysum[:, :, t, pl.ds(0, 8, stride=2), :].reshape(256, 128)
        part = dot(left, rz_mat[128 * t : 128 * t + 128, :])
        total = part if total is None else total + part
    total = total.reshape(4, 8, 8, 256)
    km[0:3] = 0.5 * total[0:3]
    km[3] = 0.125 * total[3]

    @pl.loop(1, 7)
    def _(k):
        own, inverse = centre_terms(km[3, k - 1], km[3, k], km[3, k + 1])
        cen1[k] = own
        dinv1[k] = inverse
        for c in range(3):
            m_a[c, k] = inverse * km[c, k]

    @pl.loop(0, 2)
    def _(b):
        x = 2 * b + 2
        apply = functools.partial(
            operate, lambda c, k: m_a[c, k], lambda k: km[3, k], lambda k: cen1[k]
        )
        first, second = apply(x), apply(x + 1)
        for c in range(3):
            both = (km[c, x] - first[c]) + (km[c, x + 1] - second[c])
            tlow[2 * c + b] = both[:, 0:128]

    place = iota((128, 384), 1) - 24 * gz
    halves = jnp.where((place & 1) == iota((128, 384), 0) // 64, 1.0 / 16.0, 0.0)
    spread = dot(tlow[...].reshape(48, 128), halves)
    place = iota((48, 384), 1) - 24 * gz
    row48 = iota((48, 384), 0)
    keep = (place >= 0) & (place < 24) & ((place // 4) == (row48 // 8))
    keep = keep & ((row48 % 8) // 2 == (place // 2) % 2) & (row48 % 8 < 4)
    own_g = jnp.sum(jnp.where(keep, spread, 0.0), axis=0, keepdims=True)
    gsend[...] = own_g
    round_b = [send(gsend, grecv.at[k], d) for k, d in enumerate(column)]

    low = iota((8, 128), 0) < 4
    for side, (at, extra) in enumerate(((0, 0), (0, 8))):
        total = jnp.zeros((8, 128), F32)
        for f in range(4):
            for x in range(4):
                s = 4 * f + x
                moved = pltpu.roll(km[f, 2 + x, :, 0:128], (8 * s + extra) % 128, 1)
                total = jnp.where(slot8 == s, moved, total)
        mpack[side] = jnp.where(low, total, pltpu.roll(total, 4, 0))
    round_c = []
    mid_x = {-1: slice(8, 12), 0: slice(4, 8), 1: slice(0, 4)}
    mid_row = {-1: slice(4, 8), 0: slice(0, 4), 1: slice(12, 16)}
    block = km.at[:, 2:6, 0:4, 0:128]
    for d in flat:
        round_c.append(send(block, wd.at[:, mid_x[d[0]], mid_row[d[1]], 0:128], d))
    for d in near:
        if d[2] != 0:
            side = 0 if d[2] < 0 else 1
            round_c.append(send(mpack.at[side], mrecv.at[side, 1 - d[0], 1 - d[1]], d))
    for f in range(4):
        wd[f, 4:8, 0:4, 0:128] = km[f, 2:6, 0:4, 0:128]
        wd[f, :, 8:12, 0:128] = jnp.zeros((12, 4, 128), F32)
    for copy in round_c:
        copy.wait_recv()
    for ox in range(3):
        near_y = [jnp.where(low, mrecv[side, ox, 1], mrecv[side, ox, 2]) for side in range(2)]
        far_y = [mrecv[side, ox, 0] for side in range(2)]
        for f in range(4):
            for x in range(4):
                s = 4 * f + x
                wd[f, 4 * ox + x, 0:8, 128:256] = rim(near_y[0], near_y[1], s)
                wd[f, 4 * ox + x, 8:16, 128:256] = rim(far_y[0], far_y[1], s)
    row16 = iota((16, 256), 0)
    lane16 = iota((16, 256), 1)
    y_at = gy * 4 + jnp.where(row16 < 8, row16, row16 - 16)
    z_at = gz * 128 + jnp.where(lane16 < 192, lane16, lane16 - 256)
    inside = (y_at >= 0) & (y_at < 4 * ng[1]) & (z_at >= 0) & (z_at < 128 * ng[2])
    inside = inside & ((row16 < 8) | (row16 >= 12)) & ((lane16 < 136) | (lane16 >= 248))
    inside = jnp.where(inside, 1, 0)

    @pl.loop(0, 12)
    def _(x):
        x_at = gx * 4 + x - 4
        x_in = jnp.where((x_at >= 0) & (x_at < 4 * ng[0]), 1, 0)
        wd[3, x] = jnp.where(inside * x_in > 0, wd[3, x], 0.0)

    @pl.loop(1, 11)
    def _(x):
        own, inverse = centre_terms(wd[3, x - 1], wd[3, x], wd[3, x + 1])
        cenw[x] = own
        dinvw[x] = inverse
        for c in range(3):
            m_b[c, x] = inverse * wd[c, x]

    for copy in loads[2:]:
        copy.wait()
    for copy in round_b:
        copy.wait_recv()
    g = own_g
    for k in range(len(column)):
        g = g + grecv[k]
    g = jnp.broadcast_to(g, (8, g.shape[1]))
    w = lax.dot_general(
        g, rows[...], (((1,), (1,)), ((), ())), precision=HIGH, preferred_element_type=F32
    )
    col = iota((16, 128), 1)
    blk = col // 24
    keep = (col < 72) & ((col % 24) // 2 == iota((16, 128), 0))
    keep = keep & ((blk != 0) | (gz > 0)) & ((blk != 2) | (gz < ng[2] - 1))
    picked = jnp.where(keep, jnp.broadcast_to(w[0:1, :], (16, 128)), 0.0)
    col = iota((128, 256), 0)
    quarter = iota((128, 256), 1) // 64
    code = 2 * (col // 24) + (col % 2)
    sel = jnp.where(code == jnp.where(quarter == 3, 1, quarter + 2), 1.0, 0.0)
    vown[...] = dot(picked, sel)
    round_d = [send(vown, vrecv.at[1 - d[0], 1 - d[1]], d) for d in flat]
    for copy in round_d:
        copy.wait_recv()

    row_in_8 = iota((8, 256), 0)
    for ox in range(3):
        x_at = gx + (ox - 1)
        x_in = (x_at >= 0) & (x_at < ng[0])
        values = []
        for oy in range(3):
            y_at = gy + (oy - 1)
            factor = jnp.where(x_in & (y_at >= 0) & (y_at < ng[1]), 1.0, 0.0)
            source = vown[...] if (ox, oy) == (1, 1) else vrecv[ox, oy]
            values.append(source * factor)
        for xb in range(2):
            for c in range(3):
                r = 4 * c + 2 * xb

                def line(oy, k, r=r, values=values):
                    return jnp.broadcast_to(values[oy][r + k : r + k + 1, :], (8, 256))

                upper_tile = jnp.where(
                    row_in_8 < 4,
                    jnp.where(row_in_8 < 2, line(1, 0), line(1, 1)),
                    jnp.where(row_in_8 < 6, line(2, 0), line(2, 1)),
                )
                lower_tile = jnp.where(row_in_8 < 6, line(0, 0), line(0, 1))
                for x in (4 * ox + 2 * xb, 4 * ox + 2 * xb + 1):
                    if 1 <= x < 11:
                        m_b[c, x, 0:8] += upper_tile
                        m_b[c, x, 8:16] += lower_tile

    @pl.loop(2, 10)
    def _(x):
        image = operate(lambda c, k: m_b[c, k], lambda k: wd[3, k], lambda k: cenw[k], x)
        for c in range(3):
            value = m_b[c, x] + dinvw[x] * (wd[c, x] - image[c])
            u8[c, x - 2] = jnp.where(row_in_8 < 6, value[0:8], value[8:16])

    fine_u = lax.dot_general(
        u8[...].reshape(192, 256), rz_mat[...], (((1,), (1,)), ((), ())),
        precision=HIGH, preferred_element_type=F32,
    ).reshape(3, 8, 8, 384)
    for t in range(3):
        piece = fine_u[:, :, :, 128 * t : 128 * t + 128]
        ysum[0:3, :, t, pl.ds(0, 8, stride=2), :] = piece
        ysum[0:3, :, t, pl.ds(1, 8, stride=2), :] = piece

    @pl.loop(1, 15)
    def _(x):
        k = x // 2
        for c in range(3):
            for t in range(3):
                lanes = slice(128 * t, 128 * t + 128)
                s_a[c, x, :, lanes] = s_b[c, x, :, lanes] + ysum[c, k, t]

    sweep(s_a, s_b, 2, 14)
    sweep(s_b, s_a, 3, 13)

    def last(x, sums):
        image = fine(s_a)(x + 4)
        new = list(sums)
        for c in range(3):
            p = s_a[c, x + 4, 0:8, 0:256]
            ap = image[c][0:8, 0:256]
            d = pdir[c, x]
            q = pimg[c, x]
            p_out[c, x] = p
            ap_out[c, x] = ap
            terms = (res[c, x + 4, 0:8, 0:256] * p, p * ap, p * q + d * ap, d * q)
            new = [a + b for a, b in zip(new, terms)]
        return tuple(new)

    zero = jnp.zeros((8, 256), F32)
    sums = lax.fori_loop(0, 8, last, (zero, zero, zero, zero))
    mine = jnp.zeros((8, 128), F32)
    for i, value in enumerate(sums):
        value = jnp.sum(value[:, 0:128] + value[:, 128:256], axis=0, keepdims=True)
        mine = jnp.where(row8 == i, jnp.broadcast_to(value, (8, 128)), mine)

    dsend[...] = mine
    copies = [send(dsend, drecv.at[k], d) for k, d in enumerate(layer)]
    for copy in copies:
        copy.wait_recv()
    for k in range(len(layer)):
        mine = mine + drecv[k]
    esend[...] = mine
    copies = [send(esend, erecv.at[k], d) for k, d in enumerate(column)]
    for copy in copies:
        copy.wait_recv()
    for k in range(len(column)):
        mine = mine + erecv[k]
    whole = jnp.broadcast_to(jnp.sum(mine, axis=1, keepdims=True), (8, 128))
    inner_rz, pp, cross, qq = (jnp.broadcast_to(whole[i : i + 1], (8, 128)) for i in range(4))
    beta = inner_rz / prev_rz[0]
    alpha = inner_rz / (pp + beta * (cross + beta * qq))
    ab_out[...] = jnp.where(row8 == 0, alpha, beta)
    for copy in started:
        copy.wait_send()


def solution(mesh):
    ng = tuple(mesh.shape[a] for a in AXES)

    def on_device(sol, res, pdir, pimg, prev_rz, dens, table, inverse):
        f = functools.partial(pltpu.VMEM, dtype=F32)

        def vm(*shape):
            return pltpu.VMEM(shape, F32)

        kc = inverse.shape[3]
        n_layer, n_col = ng[0] * ng[1] - 1, ng[2] - 1
        copies = 16 + 18 + 26 + 8 + n_layer + 2 * n_col
        scratch = [
            pltpu.VMEM((8, 8, 256), jnp.int32),
            vm(3, 16, 16, 384),
            vm(18, 24, 384),
            vm(18, 24, 384),
            vm(16, 16, 384), vm(16, 16, 384), vm(16, 16, 384),
            vm(3, 16, 16, 384), vm(3, 16, 16, 384),
            vm(3, 8, 8, 256), vm(3, 8, 8, 256),
            vm(2, 2, 8, 128), vm(2, 3, 3, 2, 8, 128),
            vm(4, 8, 3, 16, 128),
            vm(4, 8, 8, 256), vm(8, 8, 256), vm(8, 8, 256), vm(3, 8, 8, 256),
            vm(6, 8, 128),
            vm(2, 8, 128), vm(2, 3, 3, 8, 128),
            vm(4, 12, 16, 256), vm(12, 16, 256), vm(12, 16, 256),
            vm(3, 12, 16, 256), vm(8, 128), vm(3, 8, 8, 256),
            vm(384, 256),
            vm(1, kc), vm(n_col, 1, kc), vm(128, kc),
            vm(16, 256), vm(3, 3, 16, 256),
            vm(8, 128), vm(n_layer, 8, 128), vm(8, 128), vm(n_col, 8, 128),
            pltpu.SemaphoreType.DMA((7,)),
            pltpu.SemaphoreType.DMA((copies,)),
            pltpu.SemaphoreType.DMA((copies,)),
        ]
        anywhere = pl.BlockSpec(memory_space=pl.ANY)
        in_smem = pl.BlockSpec(memory_space=pltpu.SMEM)
        in_vmem = pl.BlockSpec(memory_space=pltpu.VMEM)
        field = jax.ShapeDtypeStruct(res.shape, F32)
        p, ap, ab = pl.pallas_call(
            functools.partial(kernel, ng),
            name="cg_step",
            out_shape=(field, field, jax.ShapeDtypeStruct((8, 128), F32)),
            in_specs=[anywhere] * 5 + [in_smem] * 2,
            out_specs=(in_vmem, in_vmem, in_vmem),
            scratch_shapes=scratch,
            compiler_params=pltpu.CompilerParams(
                collective_id=0, has_side_effects=True, vmem_limit_bytes=40 << 20
            ),
        )(res, pdir, pimg, dens, inverse, table, prev_rz.reshape(1))
        alpha, beta = ab[0, 0], ab[1, 0]
        direction = p + beta * pdir
        image = ap + beta * pimg
        return sol + alpha * direction, res - alpha * image, direction, image

    split = P(None, *AXES)
    return jax.shard_map(
        on_device,
        mesh=mesh,
        in_specs=(split, split, split, split, P(), P(*AXES), P(), P("gx", "gy", None, None)),
        out_specs=(split, split, split, split),
        check_vma=False,
    )
```

```python
import functools
import itertools
import math

import jax
import jax.numpy as jnp
from jax import lax
from jax.experimental import pallas as pl
from jax.experimental.pallas import tpu as pltpu
from jax.sharding import PartitionSpec as P


MESH = pl.DeviceIdType.MESH
AXES = ("gx", "gy", "gz")
F32 = jnp.float32
HIGH = lax.Precision.HIGHEST
DAMP = 0.6
UNROLL = 2
EIGHTIETH = 0.0125
SMALL = (-1, 0, 1)


def iota(shape, dim):
    return lax.broadcasted_iota(jnp.int32, shape, dim)


def smooth_rows_lanes(v):
    rows, lanes = v.shape
    v = (v + v) + (pltpu.roll(v, 1, 0) + pltpu.roll(v, rows - 1, 0))
    return (v + v) + (pltpu.roll(v, 1, 1) + pltpu.roll(v, lanes - 1, 1))


def three(low, mid, high):
    return (mid + mid) + (low + high)


def operate(field, coeff, centre, at):
    e_low, e_mid, e_high = coeff(at - 1), coeff(at), coeff(at + 1)
    own = centre(at)
    parts = []
    for c in range(3):
        low, mid, high = field(c, at - 1), field(c, at), field(c, at + 1)
        plain = smooth_rows_lanes(three(low, mid, high))
        scaled = smooth_rows_lanes(three(e_low * low, e_mid * mid, e_high * high))
        parts.append(own * mid - EIGHTIETH * (e_mid * plain + scaled))
    shared = 0.3 * (parts[0] + parts[1] + parts[2])
    return [0.7 * part + shared for part in parts]


def centre_terms(low, mid, high):
    wide = EIGHTIETH * smooth_rows_lanes(three(low, mid, high))
    inverse = jnp.where(mid > 0.0, DAMP / (0.7 * mid + wide), 0.0)
    return 0.9 * mid + wide, inverse


def dot(a, b):
    return jnp.dot(a, b, precision=HIGH, preferred_element_type=F32)


def kernel(
    ng,
    res_hbm, dir_hbm, img_hbm, dens_hbm, inv_hbm, table_hbm, rz_hbm,
    p_hbm, ap_hbm, ab_out,
    dens, res, ewide, e16, cen, dinv, s_a, s_b, pdir, pimg,
    spack, srecv, ysum, km, cen1, dinv1, m_a, tlow,
    mpack, mrecv, wd, cenw, dinvw, m_b, m_c, u8,
    rz_mat, sel, gsend, grecv, rows, wsend, wrecv,
    dsend, drecv, esend, erecv, p_out, ap_out, table, prev_rz,
    lsem, sems, recs,
):
    gx, gy, gz = (lax.axis_index(a) for a in AXES)
    me = (gx, gy, gz)

    def device(d):
        return tuple(lax.rem(me[i] + (d[i] % ng[i]), ng[i]) for i in range(3))

    def hops(d):
        return sum(min(d[i] % ng[i], -d[i] % ng[i]) for i in range(3))

    near = [d for d in itertools.product(SMALL, repeat=3) if d != (0, 0, 0)]
    near.sort(key=hops, reverse=True)
    flat = [d for d in near if d[2] == 0]
    tilted = [d for d in near if d[2] != 0]
    column = sorted(((0, 0, k) for k in range(1, ng[2])), key=hops, reverse=True)
    layer = [(i, j, 0) for i in range(ng[0]) for j in range(ng[1]) if (i, j) != (0, 0)]
    layer.sort(key=hops, reverse=True)
    partners = []
    for d in near + column + layer:
        d = tuple(d[i] % ng[i] for i in range(3))
        if d not in partners:
            partners.append(d)

    loads = [
        pltpu.make_async_copy(dens_hbm, dens, lsem.at[0]),
        pltpu.make_async_copy(res_hbm, res.at[:, 4:12, 0:8, 0:256], lsem.at[1]),
        pltpu.make_async_copy(dir_hbm, pdir, lsem.at[2]),
        pltpu.make_async_copy(img_hbm, pimg, lsem.at[3]),
        pltpu.make_async_copy(rz_hbm, prev_rz, lsem.at[8]),
    ]
    table_load = pltpu.make_async_copy(table_hbm, table, lsem.at[7])
    table_load.start()
    for b in range(3):
        block = jnp.clip(gz + (b - 1), 0, ng[2] - 1)
        start = pl.multiple_of(block * 24, 8)
        loads.append(
            pltpu.make_async_copy(
                inv_hbm.at[0, 0, pl.ds(start, 24), :], rows.at[24 * b : 24 * b + 24, :], lsem.at[4 + b]
            )
        )
    for copy in loads:
        copy.start()
    barrier = pltpu.get_barrier_semaphore()
    for d in partners:
        pl.semaphore_signal(barrier, inc=1, device_id=device(d), device_id_type=MESH)
    rows[72:128, :] = jnp.zeros((56, rows.shape[1]), F32)
    table_load.wait()
    loads[0].wait()

    @pl.loop(0, 8, unroll=4)
    def _(x):
        index = dens[x]
        young = jnp.full(index.shape, table[0], F32)
        for level in range(1, table.shape[0]):
            young = jnp.where(index == level, table[level], young)
        ewide[5 + x, 8:16, 0:256] = young

    loads[1].wait()

    lane8 = iota((8, 128), 1)
    row8 = iota((8, 128), 0)
    slot8 = lane8 // 8

    def fine_tile(f, x, at):
        if f < 3:
            return res[f, 4 + x, 0:8, at : at + 128]
        return ewide[5 + x, 8:16, at : at + 128]

    for side, (at, extra) in enumerate(((0, 0), (128, 8))):
        for t in range(2):
            total = jnp.zeros((8, 128), F32)
            for k in range(2):
                for x in range(8):
                    s = k * 8 + x
                    moved = pltpu.roll(fine_tile(2 * t + k, x, at), (8 * s + extra) % 128, 1)
                    total = jnp.where(slot8 == s, moved, total)
            spack[side, t] = total

    pl.semaphore_wait(barrier, len(partners))

    started = []
    counter = [0]

    def send(src, dst, d):
        k = counter[0]
        counter[0] = k + 1
        copy = pltpu.make_async_remote_copy(
            src_ref=src, dst_ref=dst, send_sem=sems.at[k], recv_sem=recs.at[k],
            device_id=device(d), device_id_type=MESH,
        )
        copy.start()
        started.append(copy)
        return copy

    pick = {
        -1: (slice(4, 8), slice(12, 16)), 0: (slice(4, 12), slice(4, 12)), 1: (slice(8, 12), slice(0, 4)),
    }
    pick_row = {-1: (slice(0, 4), slice(8, 12)), 0: (slice(0, 8), slice(0, 8)), 1: (slice(4, 8), slice(12, 16))}
    pick_e = {
        -1: (slice(5, 10), slice(13, 18)), 0: (slice(5, 13), slice(5, 13)), 1: (slice(8, 13), slice(0, 5)),
    }
    pick_e_row = {
        -1: (slice(8, 13), slice(16, 21)), 0: (slice(8, 16), slice(8, 16)), 1: (slice(11, 16), slice(3, 8)),
    }
    main = slice(0, 256)
    round_z, round_e, round_r = [], [], []
    for d in tilted:
        side = 0 if d[2] < 0 else 1
        round_z.append(send(spack.at[side], srecv.at[side, 1 - d[0], 1 - d[1]], d))
    for d in flat:
        src = ewide.at[pick_e[d[0]][0], pick_e_row[d[1]][0], main]
        dst = ewide.at[pick_e[d[0]][1], pick_e_row[d[1]][1], main]
        round_e.append(send(src, dst, d))
    for d in flat:
        src = res.at[:, pick[d[0]][0], pick_row[d[1]][0], main]
        dst = res.at[:, pick[d[0]][1], pick_row[d[1]][1], main]
        round_r.append(send(src, dst, d))

    lane_of = iota((384, 256), 0)
    target = jnp.where(lane_of < 320, lane_of // 2, lane_of // 2 + 64)
    rz_mat[...] = jnp.where(iota((384, 256), 1) == target, 1.0, 0.0)

    col = iota((128, 256), 0)
    quarter = iota((128, 256), 1) // 64
    code = 2 * (col // 24) + (col % 2)
    sel[...] = jnp.where(code == jnp.where(quarter == 3, 1, quarter + 2), 1.0, 0.0)

    for copy in round_z:
        copy.wait_recv()

    def rim(right, left, s):
        to_right = pltpu.roll(right, (-8 * s) % 128, 1)
        to_left = pltpu.roll(left, (-8 * s - 8) % 128, 1)
        return jnp.where(lane8 < 64, to_right, to_left)

    rim_lanes = slice(256, 384)
    for ox, first, count, base in ((-1, 4, 4, 0), (0, 0, 8, 4), (1, 0, 4, 12)):
        for t in range(2):
            tiles = [srecv[side, ox + 1, 1, t] for side in range(2)]
            mixed = [
                jnp.where(row8 < 4, srecv[side, ox + 1, 2, t], srecv[side, ox + 1, 0, t]) for side in range(2)
            ]

            for i in range(count):
                for k in range(2):
                    if 2 * t + k < 3:
                        s = k * 8 + first + i
                        res[2 * t + k, base + i, 0:8, rim_lanes] = rim(tiles[0], tiles[1], s)
                        res[2 * t + k, base + i, 8:16, rim_lanes] = rim(mixed[0], mixed[1], s)

    for ox, first, count, base in ((-1, 3, 5, 0), (0, 0, 8, 5), (1, 0, 5, 13)):
        tiles = [[srecv[side, ox + 1, oy, 1] for side in range(2)] for oy in range(3)]

        for i in range(count):
            for oy in range(3):
                ewide[base + i, 8 * oy : 8 * oy + 8, rim_lanes] = rim(tiles[oy][0], tiles[oy][1], 8 + first + i)

    row24 = iota((24, 384), 0)
    lane24 = iota((24, 384), 1)
    y_at = gy * 8 + row24 - 8
    z_at = gz * 256 + jnp.where(lane24 < 320, lane24, lane24 - 384)
    inside = (y_at >= 0) & (y_at < 8 * ng[1]) & (z_at >= 0) & (z_at < 256 * ng[2])
    inside = inside & ((lane24 < 264) | (lane24 >= 376)) & (row24 >= 3) & (row24 < 21)
    inside = jnp.where(inside, 1, 0)
    for copy in round_e:
        copy.wait_recv()
    upper = iota((8, 384), 0) < 4

    def fold(value):
        return jnp.concatenate([value[8:16], jnp.where(upper, value[16:24], value[0:8])], axis=0)

    def masked(x):
        x_at = gx * 8 + x - 5
        x_in = jnp.where((x_at >= 0) & (x_at < 8 * ng[0]), 1, 0)
        return jnp.where(inside * x_in > 0, ewide[x], 0.0)

    @pl.loop(0, 16, unroll=2)
    def _(x):
        low, mid, high = masked(x), masked(x + 1), masked(x + 2)
        wide = three(low, mid, high)
        wide = fold((wide + wide) + (pltpu.roll(wide, 1, 0) + pltpu.roll(wide, 23, 0)))
        wide = EIGHTIETH * ((wide + wide) + (pltpu.roll(wide, 1, 1) + pltpu.roll(wide, 383, 1)))
        mid = fold(mid)
        inverse = jnp.where(mid > 0.0, DAMP / (0.7 * mid + wide), 0.0)
        e16[x] = mid
        cen[x] = 0.9 * mid + wide
        dinv[x] = inverse

    for copy in round_r:
        copy.wait_recv()

    @pl.loop(0, 16, unroll=4)
    def _(x):
        for c in range(3):
            s_a[c, x] = dinv[x] * res[c, x]

    def fine(ref):
        return functools.partial(
            operate, lambda c, x: ref[c, x], lambda x: e16[x], lambda x: cen[x]
        )

    def sweep(source, out, start, stop):
        @pl.loop(start, stop, unroll=UNROLL)
        def _(x):
            image = fine(source)(x)
            for c in range(3):
                out[c, x] = source[c, x] + dinv[x] * (res[c, x] - image[c])

    sweep(s_a, s_b, 1, 15)

    def put_tiles(ref, f, k, value):
        for t in range(3):
            ref[f, k, t] = value[:, 128 * t : 128 * t + 128]

    @pl.loop(0, 6)
    def _(k):
        x = 2 * k + 2
        first, second = fine(s_b)(x), fine(s_b)(x + 1)
        for c in range(3):
            both = (res[c, x] - first[c]) + (res[c, x + 1] - second[c])
            put_tiles(ysum, c, k + 1, both + pltpu.roll(both, 15, 0))

    @pl.loop(0, 8, unroll=4)
    def _(k):
        both = e16[2 * k] + e16[2 * k + 1]
        put_tiles(ysum, 3, k, both + pltpu.roll(both, 15, 0))

    for c in range(3):
        for k in (0, 7):
            ysum[c, k] = jnp.zeros((3, 16, 128), F32)

    total = None
    for t in range(3):
        left = ysum[:, :, t, pl.ds(0, 8, stride=2), :].reshape(256, 128)
        part = dot(left, rz_mat[128 * t : 128 * t + 128, :])
        total = part if total is None else total + part
    total = total.reshape(4, 8, 8, 256)
    km[0:3] = 0.5 * total[0:3]
    km[3] = 0.125 * total[3]

    @pl.loop(1, 7, unroll=3)
    def _(k):
        own, inverse = centre_terms(km[3, k - 1], km[3, k], km[3, k + 1])
        cen1[k] = own
        dinv1[k] = inverse
        for c in range(3):
            m_a[c, k] = inverse * km[c, k]

    @pl.loop(0, 2)
    def _(b):
        x = 2 * b + 2
        apply = functools.partial(
            operate, lambda c, k: m_a[c, k], lambda k: km[3, k], lambda k: cen1[k]
        )
        first, second = apply(x), apply(x + 1)
        for c in range(3):
            both = (km[c, x] - first[c]) + (km[c, x + 1] - second[c])
            tlow[2 * c + b] = both[:, 0:128]

    place = iota((128, 384), 1) - 24 * gz
    halves = jnp.where((place & 1) == iota((128, 384), 0) // 64, 1.0 / 16.0, 0.0)
    spread = dot(tlow[...].reshape(48, 128), halves)
    place = iota((48, 384), 1) - 24 * gz
    row48 = iota((48, 384), 0)
    keep = (place >= 0) & (place < 24) & ((place // 4) == (row48 // 8))
    keep = keep & ((row48 % 8) // 2 == (place // 2) % 2) & (row48 % 8 < 4)
    own_g = jnp.sum(jnp.where(keep, spread, 0.0), axis=0, keepdims=True)
    gsend[...] = own_g
    round_b = [send(gsend, grecv.at[k], d) for k, d in enumerate(column)]

    low = iota((8, 128), 0) < 4
    for side, (at, extra) in enumerate(((0, 0), (0, 8))):
        total = jnp.zeros((8, 128), F32)
        for f in range(4):
            for x in range(4):
                s = 4 * f + x
                moved = pltpu.roll(km[f, 2 + x, :, 0:128], (8 * s + extra) % 128, 1)
                total = jnp.where(slot8 == s, moved, total)
        mpack[side] = jnp.where(low, total, pltpu.roll(total, 4, 0))
    round_c = []
    mid_x = {-1: slice(8, 12), 0: slice(4, 8), 1: slice(0, 4)}
    mid_row = {-1: slice(4, 8), 0: slice(0, 4), 1: slice(12, 16)}
    block = km.at[:, 2:6, 0:4, 0:128]
    for d in flat:
        round_c.append(send(block, wd.at[:, mid_x[d[0]], mid_row[d[1]], 0:128], d))
    for d in tilted:
        side = 0 if d[2] < 0 else 1
        round_c.append(send(mpack.at[side], mrecv.at[side, 1 - d[0], 1 - d[1]], d))
    for f in range(4):
        wd[f, 4:8, 0:4, 0:128] = km[f, 2:6, 0:4, 0:128]
        wd[f, :, 8:12, 0:128] = jnp.zeros((12, 4, 128), F32)
    for copy in loads[2:]:
        copy.wait()
    for copy in round_b:
        copy.wait_recv()
    g = own_g
    for k in range(len(column)):
        g = g + grecv[k]
    g = jnp.broadcast_to(g, (8, g.shape[1]))
    w = lax.dot_general(
        g, rows[...], (((1,), (1,)), ((), ())), precision=HIGH, preferred_element_type=F32
    )
    wsend[...] = w[0:1, :]
    round_d = [send(wsend, wrecv.at[1 - d[0], 1 - d[1]], d) for d in flat]

    for copy in round_c:
        copy.wait_recv()
    for ox in range(3):
        near_y = [jnp.where(low, mrecv[side, ox, 1], mrecv[side, ox, 2]) for side in range(2)]
        far_y = [mrecv[side, ox, 0] for side in range(2)]
        for f in range(4):
            for x in range(4):
                s = 4 * f + x
                wd[f, 4 * ox + x, 0:8, 128:256] = rim(near_y[0], near_y[1], s)
                wd[f, 4 * ox + x, 8:16, 128:256] = rim(far_y[0], far_y[1], s)
    row16 = iota((16, 256), 0)
    lane16 = iota((16, 256), 1)
    y_at = gy * 4 + jnp.where(row16 < 8, row16, row16 - 16)
    z_at = gz * 128 + jnp.where(lane16 < 192, lane16, lane16 - 256)
    inside = (y_at >= 0) & (y_at < 4 * ng[1]) & (z_at >= 0) & (z_at < 128 * ng[2])
    inside = inside & ((row16 < 8) | (row16 >= 12)) & ((lane16 < 136) | (lane16 >= 248))
    inside = jnp.where(inside, 1, 0)

    @pl.loop(0, 12, unroll=4)
    def _(x):
        x_at = gx * 4 + x - 4
        x_in = jnp.where((x_at >= 0) & (x_at < 4 * ng[0]), 1, 0)
        wd[3, x] = jnp.where(inside * x_in > 0, wd[3, x], 0.0)

    @pl.loop(1, 11, unroll=2)
    def _(x):
        own, inverse = centre_terms(wd[3, x - 1], wd[3, x], wd[3, x + 1])
        cenw[x] = own
        dinvw[x] = inverse
        for c in range(3):
            m_b[c, x] = inverse * wd[c, x]

    col = iota((16, 128), 1)
    blk = col // 24
    keep = (col < 72) & ((col % 24) // 2 == iota((16, 128), 0))
    keep = keep & ((blk != 0) | (gz > 0)) & ((blk != 2) | (gz < ng[2] - 1))
    for copy in round_d:
        copy.wait_recv()
    picked = []
    for ox in range(3):
        for oy in range(3):
            x_at, y_at = gx + (ox - 1), gy + (oy - 1)
            known = (x_at >= 0) & (x_at < ng[0]) & (y_at >= 0) & (y_at < ng[1])
            line = wsend[...] if (ox, oy) == (1, 1) else wrecv[ox, oy]
            line = jnp.broadcast_to(line * jnp.where(known, 1.0, 0.0), (16, 128))
            picked.append(jnp.where(keep, line, 0.0))
    blocks = dot(jnp.concatenate(picked, axis=0), sel[...])

    row_in_8 = iota((8, 256), 0)
    for ox in range(3):
        values = [blocks[16 * (3 * ox + oy) : 16 * (3 * ox + oy) + 16] for oy in range(3)]
        for xb in range(2):
            for c in range(3):
                r = 4 * c + 2 * xb

                def line(oy, k, r=r, values=values):
                    return jnp.broadcast_to(values[oy][r + k : r + k + 1, :], (8, 256))

                upper_tile = jnp.where(
                    row_in_8 < 4,
                    jnp.where(row_in_8 < 2, line(1, 0), line(1, 1)),
                    jnp.where(row_in_8 < 6, line(2, 0), line(2, 1)),
                )
                lower_tile = jnp.where(row_in_8 < 6, line(0, 0), line(0, 1))
                for x in (4 * ox + 2 * xb, 4 * ox + 2 * xb + 1):
                    if 1 <= x < 11:
                        m_b[c, x, 0:8] += upper_tile
                        m_b[c, x, 8:16] += lower_tile

    @pl.loop(2, 10, unroll=UNROLL)
    def _(x):
        image = operate(lambda c, k: m_b[c, k], lambda k: wd[3, k], lambda k: cenw[k], x)
        for c in range(3):
            value = m_b[c, x] + dinvw[x] * (wd[c, x] - image[c])
            u8[c, x - 2] = jnp.where(row_in_8 < 6, value[0:8], value[8:16])

    fine_u = lax.dot_general(
        u8[...].reshape(192, 256), rz_mat[...], (((1,), (1,)), ((), ())),
        precision=HIGH, preferred_element_type=F32,
    ).reshape(3, 8, 8, 384)
    for t in range(3):
        piece = fine_u[:, :, :, 128 * t : 128 * t + 128]
        ysum[0:3, :, t, pl.ds(0, 8, stride=2), :] = piece
        ysum[0:3, :, t, pl.ds(1, 8, stride=2), :] = piece

    @pl.loop(1, 15, unroll=2)
    def _(x):
        k = x // 2
        for c in range(3):
            for t in range(3):
                lanes = slice(128 * t, 128 * t + 128)
                s_a[c, x, :, lanes] = s_b[c, x, :, lanes] + ysum[c, k, t]

    sweep(s_a, s_b, 2, 14)
    sweep(s_b, s_a, 3, 13)

    def last(x, sums):
        image = fine(s_a)(x + 4)
        new = list(sums)
        for c in range(3):
            p = s_a[c, x + 4, 0:8, 0:256]
            ap = image[c][0:8, 0:256]
            d = pdir[c, x]
            q = pimg[c, x]
            p_out[c, x] = p
            ap_out[c, x] = ap
            terms = (res[c, x + 4, 0:8, 0:256] * p, p * ap, p * q + d * ap, d * q)
            new = [a + b for a, b in zip(new, terms)]
        return tuple(new)

    zero = jnp.zeros((8, 256), F32)
    stores = [
        pltpu.make_async_copy(p_out, p_hbm, lsem.at[0]),
        pltpu.make_async_copy(ap_out, ap_hbm, lsem.at[1]),
    ]
    sums = lax.fori_loop(0, 8, last, (zero, zero, zero, zero), unroll=UNROLL)
    group = iota((1, 128), 1) // 32
    mine = jnp.zeros((1, 128), F32)
    for i, value in enumerate(sums):
        value = jnp.sum(value[:, 0:128] + value[:, 128:256], axis=0, keepdims=True)
        value = value + pltpu.roll(value, 64, 1)
        value = value + pltpu.roll(value, 32, 1)
        mine = jnp.where(group == i, value, mine)

    for peers, out, into in ((layer, dsend, drecv), (column, esend, erecv)):
        out[...] = mine
        copies = [send(out, into.at[k], d) for k, d in enumerate(peers)]
        if peers is layer:
            for copy in stores:
                copy.start()
        for copy in copies:
            copy.wait_recv()
        for k in range(len(peers)):
            mine = mine + into[k]
    inner_rz, pp, cross, qq = (
        jnp.sum(jnp.where(group == i, mine, 0.0), axis=1, keepdims=True) for i in range(4)
    )
    beta = inner_rz / prev_rz[0]
    alpha = inner_rz / (pp + beta * (cross + beta * qq))
    ab_out[...] = jnp.where(group < 2, alpha, beta)
    for copy in stores:
        copy.wait()
    for copy in started:
        copy.wait_send()


def finish(
    *refs,
):
    sources, ab_hbm, targets = refs[0:6], refs[6], refs[7:11]
    held, ab, made, sems, outs = refs[11:17], refs[17], refs[18:22], refs[22], refs[23]
    ab_load = pltpu.make_async_copy(ab_hbm, ab, sems.at[3, 0])
    ab_load.start()
    loads = [
        [pltpu.make_async_copy(src.at[c], dst.at[c], sems.at[c, i]) for i, (src, dst) in enumerate(zip(sources, held))]
        for c in range(3)
    ]
    for part in loads:
        for copy in part:
            copy.start()
    pdir, pimg, sol, res, p, ap = held
    new_sol, new_res, new_dir, new_img = made
    ab_load.wait()
    alpha = jnp.broadcast_to(ab[0:1, 0:1], (8, 256))
    beta = jnp.broadcast_to(ab[0:1, 64:65], (8, 256))
    stores = []
    for c in range(3):
        for copy in loads[c]:
            copy.wait()
        for x in range(p.shape[1]):
            direction = p[c, x] + beta * pdir[c, x]
            image = ap[c, x] + beta * pimg[c, x]
            new_dir[c, x] = direction
            new_img[c, x] = image
            new_sol[c, x] = sol[c, x] + alpha * direction
            new_res[c, x] = res[c, x] - alpha * image
        for i, (src, dst) in enumerate(zip(made, targets)):
            copy = pltpu.make_async_copy(src.at[c], dst.at[c], outs.at[c, i])
            copy.start()
            stores.append(copy)
    for copy in stores:
        copy.wait()


def solution(mesh):
    ng = tuple(mesh.shape[a] for a in AXES)

    def on_device(sol, res, pdir, pimg, prev_rz, dens, table, inverse):
        def vm(*shape):
            return pltpu.VMEM(shape, F32)

        kc = inverse.shape[3]
        n_layer, n_col = ng[0] * ng[1] - 1, ng[2] - 1
        copies = 16 + 18 + 26 + 8 + n_layer + 2 * n_col
        scratch = [
            pltpu.VMEM((8, 8, 256), jnp.int32),
            vm(3, 16, 16, 384),
            vm(18, 24, 384),
            vm(16, 16, 384), vm(16, 16, 384), vm(16, 16, 384),
            vm(3, 16, 16, 384), vm(3, 16, 16, 384),
            vm(3, 8, 8, 256), vm(3, 8, 8, 256),
            vm(2, 2, 8, 128), vm(2, 3, 3, 2, 8, 128),
            vm(4, 8, 3, 16, 128),
            vm(4, 8, 8, 256), vm(8, 8, 256), vm(8, 8, 256), vm(3, 8, 8, 256),
            vm(6, 8, 128),
            vm(2, 8, 128), vm(2, 3, 3, 8, 128),
            vm(4, 12, 16, 256), vm(12, 16, 256), vm(12, 16, 256),
            vm(3, 12, 16, 256), vm(8, 128), vm(3, 8, 8, 256),
            vm(384, 256), vm(128, 256),
            vm(1, kc), vm(n_col, 1, kc), vm(128, kc),
            vm(1, 128), vm(3, 3, 1, 128),
            vm(1, 128), vm(n_layer, 1, 128), vm(1, 128), vm(n_col, 1, 128),
            vm(3, 8, 8, 256), vm(3, 8, 8, 256),
            pltpu.SMEM(table.shape, F32), pltpu.SMEM((1,), F32),
            pltpu.SemaphoreType.DMA((9,)),
            pltpu.SemaphoreType.DMA((copies,)),
            pltpu.SemaphoreType.DMA((copies,)),
        ]
        in_hbm = pl.BlockSpec(memory_space=pltpu.HBM)
        in_vmem = pl.BlockSpec(memory_space=pltpu.VMEM)
        field = jax.ShapeDtypeStruct(res.shape, F32)
        p, ap, ab = pl.pallas_call(
            functools.partial(kernel, ng),
            name="cg_step",
            out_shape=(field, field, jax.ShapeDtypeStruct((1, 128), F32)),
            in_specs=[in_hbm] * 7,
            out_specs=(in_hbm, in_hbm, in_vmem),
            scratch_shapes=scratch,
            compiler_params=pltpu.CompilerParams(
                collective_id=0, has_side_effects=True, vmem_limit_bytes=56 << 20
            ),
        )(res, pdir, pimg, dens, inverse, table, prev_rz.reshape(1))
        return pl.pallas_call(
            finish,
            name="cg_finish",
            out_shape=(field,) * 4,
            in_specs=[in_hbm] * 7,
            out_specs=(in_hbm,) * 4,
            scratch_shapes=[vm(*res.shape)] * 6 + [vm(1, 128)] + [vm(*res.shape)] * 4
            + [pltpu.SemaphoreType.DMA((4, 6)), pltpu.SemaphoreType.DMA((3, 4))],
            compiler_params=pltpu.CompilerParams(vmem_limit_bytes=56 << 20),
        )(pdir, pimg, sol, res, p, ap, ab)

    split = P(None, *AXES)
    return jax.shard_map(
        on_device,
        mesh=mesh,
        in_specs=(split, split, split, split, P(), P(*AXES), P(), P("gx", "gy", None, None)),
        out_specs=(split, split, split, split),
        check_vma=False,
    )
```

```python
import functools
import itertools
import math

import jax
import jax.numpy as jnp
from jax import lax
from jax.experimental import pallas as pl
from jax.experimental.pallas import tpu as pltpu
from jax.sharding import PartitionSpec as P


MESH = pl.DeviceIdType.MESH
AXES = ("gx", "gy", "gz")
F32 = jnp.float32
HIGH = lax.Precision.HIGHEST
DAMP = 0.6
UNROLL = 2
STEP = 2
EIGHTIETH = 0.0125
SMALL = (-1, 0, 1)


def iota(shape, dim):
    return lax.broadcasted_iota(jnp.int32, shape, dim)


def smooth_rows_lanes(v):
    rows, lanes = v.shape
    v = (v + v) + (pltpu.roll(v, 1, 0) + pltpu.roll(v, rows - 1, 0))
    return (v + v) + (pltpu.roll(v, 1, 1) + pltpu.roll(v, lanes - 1, 1))


def three(low, mid, high):
    return (mid + mid) + (low + high)


def operate(field, coeff, centre, at, count):
    planes = range(count + 2)
    e = [coeff(at - 1 + i) for i in planes]
    parts = [[] for _ in range(count)]
    for c in range(3):
        v = [field(c, at - 1 + i) for i in planes]
        ev = [e[i] * v[i] for i in planes]
        pair = [v[i] + v[i + 1] for i in range(count + 1)]
        epair = [ev[i] + ev[i + 1] for i in range(count + 1)]
        for i in range(count):
            plain = smooth_rows_lanes(pair[i] + pair[i + 1])
            scaled = smooth_rows_lanes(epair[i] + epair[i + 1])
            parts[i].append(centre(at + i) * v[i + 1] - EIGHTIETH * (e[i + 1] * plain + scaled))
    images = []
    for part in parts:
        shared = 0.3 * (part[0] + part[1] + part[2])
        images.append([0.7 * piece + shared for piece in part])
    return images


def centre_terms(low, mid, high):
    wide = EIGHTIETH * smooth_rows_lanes(three(low, mid, high))
    inverse = jnp.where(mid > 0.0, DAMP / (0.7 * mid + wide), 0.0)
    return 0.9 * mid + wide, inverse


def dot(a, b, dims=(((1,), (0,)), ((), ()))):
    total = None
    for part in range(3):
        piece = a.astype(jnp.bfloat16)
        term = lax.dot_general(piece, b, dims, preferred_element_type=F32)
        total = term if total is None else total + term
        if part < 2:
            a = a - piece.astype(F32)
    return total


def kernel(
    ng,
    res_hbm, dir_hbm, img_hbm, dens_hbm, inv_hbm, table_hbm, rz_hbm,
    p_hbm, ap_hbm, ab_out,
    dens, res, ewide, e16, cen, dinv, s_a, s_b, pdir, pimg,
    spack, srecv, ysum, km, cen1, dinv1, m_a, tlow,
    mpack, mrecv, wd, cenw, dinvw, m_b, m_c, u8,
    rz_mat, sel, halves, keep48, gsend, grecv, rows, wsend, wrecv,
    dsend, drecv, esend, erecv, p_out, ap_out, table, prev_rz,
    lsem, sems, recs,
):
    gx, gy, gz = (lax.axis_index(a) for a in AXES)
    me = (gx, gy, gz)

    def device(d):
        return tuple(lax.rem(me[i] + (d[i] % ng[i]), ng[i]) for i in range(3))

    def hops(d):
        return sum(min(d[i] % ng[i], -d[i] % ng[i]) for i in range(3))

    near = [d for d in itertools.product(SMALL, repeat=3) if d != (0, 0, 0)]
    near.sort(key=hops, reverse=True)
    flat = [d for d in near if d[2] == 0]
    tilted = [d for d in near if d[2] != 0]
    column = sorted(((0, 0, k) for k in range(1, ng[2])), key=hops, reverse=True)
    layer = [(i, j, 0) for i in range(ng[0]) for j in range(ng[1]) if (i, j) != (0, 0)]
    layer.sort(key=hops, reverse=True)
    partners = []
    for d in near + column + layer:
        d = tuple(d[i] % ng[i] for i in range(3))
        if d not in partners:
            partners.append(d)

    loads = [
        pltpu.make_async_copy(dens_hbm, dens, lsem.at[0]),
        pltpu.make_async_copy(res_hbm, res.at[:, 4:12, 0:8, 0:256], lsem.at[1]),
        pltpu.make_async_copy(dir_hbm, pdir, lsem.at[2]),
        pltpu.make_async_copy(img_hbm, pimg, lsem.at[3]),
        pltpu.make_async_copy(rz_hbm, prev_rz, lsem.at[8]),
    ]
    table_load = pltpu.make_async_copy(table_hbm, table, lsem.at[7])
    table_load.start()
    for b in range(3):
        block = jnp.clip(gz + (b - 1), 0, ng[2] - 1)
        start = pl.multiple_of(block * 24, 8)
        loads.append(
            pltpu.make_async_copy(
                inv_hbm.at[0, 0, pl.ds(start, 24), :], rows.at[24 * b : 24 * b + 24, :], lsem.at[4 + b]
            )
        )
    for copy in loads:
        copy.start()
    barrier = pltpu.get_barrier_semaphore()
    for d in partners:
        pl.semaphore_signal(barrier, inc=1, device_id=device(d), device_id_type=MESH)
    rows[72:128, :] = jnp.zeros((56, rows.shape[1]), F32)
    table_load.wait()
    loads[0].wait()

    @pl.loop(0, 8, unroll=4)
    def _(x):
        index = dens[x]
        young = jnp.full(index.shape, table[0], F32)
        for level in range(1, table.shape[0]):
            young = jnp.where(index == level, table[level], young)
        ewide[5 + x, 8:16, 0:256] = young

    loads[1].wait()

    lane8 = iota((8, 128), 1)
    row8 = iota((8, 128), 0)
    slot8 = lane8 // 8

    def fine_tile(f, x, at):
        if f < 3:
            return res[f, 4 + x, 0:8, at : at + 128]
        return ewide[5 + x, 8:16, at : at + 128]

    for side, (at, extra) in enumerate(((0, 0), (128, 8))):
        for t in range(2):
            total = jnp.zeros((8, 128), F32)
            for k in range(2):
                for x in range(8):
                    s = k * 8 + x
                    moved = pltpu.roll(fine_tile(2 * t + k, x, at), (8 * s + extra) % 128, 1)
                    total = jnp.where(slot8 == s, moved, total)
            spack[side, t] = total

    pl.semaphore_wait(barrier, len(partners))

    started = []
    counter = [0]

    def send(src, dst, d):
        k = counter[0]
        counter[0] = k + 1
        copy = pltpu.make_async_remote_copy(
            src_ref=src, dst_ref=dst, send_sem=sems.at[k], recv_sem=recs.at[k],
            device_id=device(d), device_id_type=MESH,
        )
        copy.start()
        started.append(copy)
        return copy

    pick = {
        -1: (slice(4, 8), slice(12, 16)), 0: (slice(4, 12), slice(4, 12)), 1: (slice(8, 12), slice(0, 4)),
    }
    pick_row = {-1: (slice(0, 4), slice(8, 12)), 0: (slice(0, 8), slice(0, 8)), 1: (slice(4, 8), slice(12, 16))}
    pick_e = {
        -1: (slice(5, 10), slice(13, 18)), 0: (slice(5, 13), slice(5, 13)), 1: (slice(8, 13), slice(0, 5)),
    }
    pick_e_row = {
        -1: (slice(8, 13), slice(16, 21)), 0: (slice(8, 16), slice(8, 16)), 1: (slice(11, 16), slice(3, 8)),
    }
    main = slice(0, 256)
    round_z, round_e, round_y, round_r = [], [], [], []
    for d in tilted:
        side = 0 if d[2] < 0 else 1
        round_z.append(send(spack.at[side], srecv.at[side, 1 - d[0], 1 - d[1]], d))
    for d in flat:
        src = ewide.at[pick_e[d[0]][0], pick_e_row[d[1]][0], main]
        dst = ewide.at[pick_e[d[0]][1], pick_e_row[d[1]][1], main]
        round_e.append(send(src, dst, d))
    for d in reversed(flat):
        src = res.at[:, pick[d[0]][0], pick_row[d[1]][0], main]
        dst = res.at[:, pick[d[0]][1], pick_row[d[1]][1], main]
        (round_y if d[0] == 0 else round_r).append(send(src, dst, d))

    lane_of = iota((384, 256), 0)
    target = jnp.where(lane_of < 320, lane_of // 2, lane_of // 2 + 64)
    rz_mat[...] = jnp.where(iota((384, 256), 1) == target, 1.0, 0.0).astype(jnp.bfloat16)
    place = iota((128, 384), 1) - 24 * gz
    halves[...] = jnp.where((place & 1) == iota((128, 384), 0) // 64, 1.0 / 16.0, 0.0).astype(jnp.bfloat16)
    place = iota((48, 384), 1) - 24 * gz
    row48 = iota((48, 384), 0)
    keep = (place >= 0) & (place < 24) & ((place // 4) == (row48 // 8))
    keep = keep & ((row48 % 8) // 2 == (place // 2) % 2) & (row48 % 8 < 4)
    keep48[...] = jnp.where(keep, 1.0, 0.0)

    col = iota((128, 256), 0)
    quarter = iota((128, 256), 1) // 64
    code = 2 * (col // 24) + (col % 2)
    sel[...] = jnp.where(code == jnp.where(quarter == 3, 1, quarter + 2), 1.0, 0.0).astype(jnp.bfloat16)

    for copy in round_z:
        copy.wait_recv()

    def rim(right, left, s):
        to_right = pltpu.roll(right, (-8 * s) % 128, 1)
        to_left = pltpu.roll(left, (-8 * s - 8) % 128, 1)
        return jnp.where(lane8 < 64, to_right, to_left)

    rim_lanes = slice(256, 384)
    for ox, first, count, base in ((-1, 4, 4, 0), (0, 0, 8, 4), (1, 0, 4, 12)):
        for t in range(2):
            tiles = [srecv[side, ox + 1, 1, t] for side in range(2)]
            mixed = [
                jnp.where(row8 < 4, srecv[side, ox + 1, 2, t], srecv[side, ox + 1, 0, t]) for side in range(2)
            ]

            for i in range(count):
                for k in range(2):
                    if 2 * t + k < 3:
                        s = k * 8 + first + i
                        res[2 * t + k, base + i, 0:8, rim_lanes] = rim(tiles[0], tiles[1], s)
                        res[2 * t + k, base + i, 8:16, rim_lanes] = rim(mixed[0], mixed[1], s)

    for ox, first, count, base in ((-1, 3, 5, 0), (0, 0, 8, 5), (1, 0, 5, 13)):
        tiles = [[srecv[side, ox + 1, oy, 1] for side in range(2)] for oy in range(3)]

        for i in range(count):
            for oy in range(3):
                ewide[base + i, 8 * oy : 8 * oy + 8, rim_lanes] = rim(tiles[oy][0], tiles[oy][1], 8 + first + i)

    row24 = iota((24, 384), 0)
    lane24 = iota((24, 384), 1)
    y_at = gy * 8 + row24 - 8
    z_at = gz * 256 + jnp.where(lane24 < 320, lane24, lane24 - 384)
    inside = (y_at >= 0) & (y_at < 8 * ng[1]) & (z_at >= 0) & (z_at < 256 * ng[2])
    inside = inside & ((lane24 < 264) | (lane24 >= 376)) & (row24 >= 3) & (row24 < 21)
    inside = jnp.where(inside, 1, 0)
    for copy in round_e:
        copy.wait_recv()
    upper = iota((8, 384), 0) < 4

    def fold(value):
        return jnp.concatenate([value[8:16], jnp.where(upper, value[16:24], value[0:8])], axis=0)

    def masked(x):
        x_at = gx * 8 + x - 5
        x_in = jnp.where((x_at >= 0) & (x_at < 8 * ng[0]), 1, 0)
        return jnp.where(inside * x_in > 0, ewide[x], 0.0)

    @pl.loop(0, 16, unroll=2)
    def _(x):
        low, mid, high = masked(x), masked(x + 1), masked(x + 2)
        wide = three(low, mid, high)
        wide = fold((wide + wide) + (pltpu.roll(wide, 1, 0) + pltpu.roll(wide, 23, 0)))
        wide = EIGHTIETH * ((wide + wide) + (pltpu.roll(wide, 1, 1) + pltpu.roll(wide, 383, 1)))
        mid = fold(mid)
        inverse = jnp.where(mid > 0.0, DAMP / (0.7 * mid + wide), 0.0)
        e16[x] = mid
        cen[x] = 0.9 * mid + wide
        dinv[x] = inverse

    def begin(start, stop):
        @pl.loop(start, stop, unroll=4)
        def _(x):
            for c in range(3):
                s_a[c, x] = dinv[x] * res[c, x]

    for copy in round_y:
        copy.wait_recv()
    begin(4, 12)

    def fine(ref):
        return functools.partial(
            operate, lambda c, x: ref[c, x], lambda x: e16[x], lambda x: cen[x]
        )

    def sweep(source, out, start, stop, count=STEP):
        assert (stop - start) % count == 0

        @pl.loop(0, (stop - start) // count, unroll=UNROLL)
        def _(k):
            x = start + count * k
            for i, image in enumerate(fine(source)(x, count)):
                for c in range(3):
                    out[c, x + i] = source[c, x + i] + dinv[x + i] * (res[c, x + i] - image[c])

    sweep(s_a, s_b, 5, 11, 2)
    for copy in round_r:
        copy.wait_recv()
    begin(0, 4)
    begin(12, 16)
    sweep(s_a, s_b, 1, 5, 2)
    sweep(s_a, s_b, 11, 15, 2)

    def put_tiles(ref, f, k, value):
        for t in range(3):
            ref[f, k, t] = value[:, 128 * t : 128 * t + 128]

    @pl.loop(0, 6)
    def _(k):
        x = 2 * k + 2
        first, second = fine(s_b)(x, 2)
        for c in range(3):
            both = (res[c, x] - first[c]) + (res[c, x + 1] - second[c])
            put_tiles(ysum, c, k + 1, both + pltpu.roll(both, 15, 0))

    @pl.loop(0, 8, unroll=4)
    def _(k):
        both = e16[2 * k] + e16[2 * k + 1]
        put_tiles(ysum, 3, k, both + pltpu.roll(both, 15, 0))

    for c in range(3):
        for k in (0, 7):
            ysum[c, k] = jnp.zeros((3, 16, 128), F32)

    total = None
    for t in range(3):
        left = ysum[:, :, t, pl.ds(0, 8, stride=2), :].reshape(256, 128)
        part = dot(left, rz_mat[128 * t : 128 * t + 128, :])
        total = part if total is None else total + part
    total = total.reshape(4, 8, 8, 256)
    km[0:3] = 0.5 * total[0:3]
    km[3] = 0.125 * total[3]

    @pl.loop(1, 7, unroll=3)
    def _(k):
        own, inverse = centre_terms(km[3, k - 1], km[3, k], km[3, k + 1])
        cen1[k] = own
        dinv1[k] = inverse
        for c in range(3):
            m_a[c, k] = inverse * km[c, k]

    @pl.loop(0, 2)
    def _(b):
        x = 2 * b + 2
        apply = functools.partial(
            operate, lambda c, k: m_a[c, k], lambda k: km[3, k], lambda k: cen1[k]
        )
        first, second = apply(x, 2)
        for c in range(3):
            both = (km[c, x] - first[c]) + (km[c, x + 1] - second[c])
            tlow[2 * c + b] = both[:, 0:128]

    spread = dot(tlow[...].reshape(48, 128), halves[...])
    own_g = jnp.sum(jnp.where(keep48[...] > 0.0, spread, 0.0), axis=0, keepdims=True)
    gsend[...] = own_g
    round_b = [send(gsend, grecv.at[k], d) for k, d in enumerate(column)]

    low = iota((8, 128), 0) < 4
    for side, (at, extra) in enumerate(((0, 0), (0, 8))):
        total = jnp.zeros((8, 128), F32)
        for f in range(4):
            for x in range(4):
                s = 4 * f + x
                moved = pltpu.roll(km[f, 2 + x, :, 0:128], (8 * s + extra) % 128, 1)
                total = jnp.where(slot8 == s, moved, total)
        mpack[side] = jnp.where(low, total, pltpu.roll(total, 4, 0))
    round_c = []
    mid_x = {-1: slice(8, 12), 0: slice(4, 8), 1: slice(0, 4)}
    mid_row = {-1: slice(4, 8), 0: slice(0, 4), 1: slice(12, 16)}
    block = km.at[:, 2:6, 0:4, 0:128]
    for d in flat:
        round_c.append(send(block, wd.at[:, mid_x[d[0]], mid_row[d[1]], 0:128], d))
    for d in tilted:
        side = 0 if d[2] < 0 else 1
        round_c.append(send(mpack.at[side], mrecv.at[side, 1 - d[0], 1 - d[1]], d))
    for f in range(4):
        wd[f, 4:8, 0:4, 0:128] = km[f, 2:6, 0:4, 0:128]
        wd[f, :, 8:12, 0:128] = jnp.zeros((12, 4, 128), F32)
    for copy in loads[2:]:
        copy.wait()
    for copy in round_b:
        copy.wait_recv()
    g = own_g
    for k in range(len(column)):
        g = g + grecv[k]
    g = jnp.broadcast_to(g, (8, g.shape[1]))
    w = lax.dot_general(
        g, rows[...], (((1,), (1,)), ((), ())), precision=HIGH, preferred_element_type=F32
    )
    wsend[...] = w[0:1, :]
    round_d = [send(wsend, wrecv.at[1 - d[0], 1 - d[1]], d) for d in flat]

    for copy in round_c:
        copy.wait_recv()
    for ox in range(3):
        near_y = [jnp.where(low, mrecv[side, ox, 1], mrecv[side, ox, 2]) for side in range(2)]
        far_y = [mrecv[side, ox, 0] for side in range(2)]
        for f in range(4):
            for x in range(4):
                s = 4 * f + x
                wd[f, 4 * ox + x, 0:8, 128:256] = rim(near_y[0], near_y[1], s)
                wd[f, 4 * ox + x, 8:16, 128:256] = rim(far_y[0], far_y[1], s)
    row16 = iota((16, 256), 0)
    lane16 = iota((16, 256), 1)
    y_at = gy * 4 + jnp.where(row16 < 8, row16, row16 - 16)
    z_at = gz * 128 + jnp.where(lane16 < 192, lane16, lane16 - 256)
    inside = (y_at >= 0) & (y_at < 4 * ng[1]) & (z_at >= 0) & (z_at < 128 * ng[2])
    inside = inside & ((row16 < 8) | (row16 >= 12)) & ((lane16 < 136) | (lane16 >= 248))
    inside = jnp.where(inside, 1, 0)

    @pl.loop(0, 12, unroll=4)
    def _(x):
        x_at = gx * 4 + x - 4
        x_in = jnp.where((x_at >= 0) & (x_at < 4 * ng[0]), 1, 0)
        wd[3, x] = jnp.where(inside * x_in > 0, wd[3, x], 0.0)

    @pl.loop(1, 11, unroll=2)
    def _(x):
        own, inverse = centre_terms(wd[3, x - 1], wd[3, x], wd[3, x + 1])
        cenw[x] = own
        dinvw[x] = inverse
        for c in range(3):
            m_b[c, x] = inverse * wd[c, x]

    col = iota((16, 128), 1)
    blk = col // 24
    keep = (col < 72) & ((col % 24) // 2 == iota((16, 128), 0))
    keep = keep & ((blk != 0) | (gz > 0)) & ((blk != 2) | (gz < ng[2] - 1))
    for copy in round_d:
        copy.wait_recv()
    picked = []
    for ox in range(3):
        for oy in range(3):
            x_at, y_at = gx + (ox - 1), gy + (oy - 1)
            known = (x_at >= 0) & (x_at < ng[0]) & (y_at >= 0) & (y_at < ng[1])
            line = wsend[...] if (ox, oy) == (1, 1) else wrecv[ox, oy]
            line = jnp.broadcast_to(line * jnp.where(known, 1.0, 0.0), (16, 128))
            picked.append(jnp.where(keep, line, 0.0))
    blocks = dot(jnp.concatenate(picked, axis=0), sel[...])

    row_in_8 = iota((8, 256), 0)
    for ox in range(3):
        values = [blocks[16 * (3 * ox + oy) : 16 * (3 * ox + oy) + 16] for oy in range(3)]
        for xb in range(2):
            for c in range(3):
                r = 4 * c + 2 * xb

                def line(oy, k, r=r, values=values):
                    return jnp.broadcast_to(values[oy][r + k : r + k + 1, :], (8, 256))

                upper_tile = jnp.where(
                    row_in_8 < 4,
                    jnp.where(row_in_8 < 2, line(1, 0), line(1, 1)),
                    jnp.where(row_in_8 < 6, line(2, 0), line(2, 1)),
                )
                lower_tile = jnp.where(row_in_8 < 6, line(0, 0), line(0, 1))
                for x in (4 * ox + 2 * xb, 4 * ox + 2 * xb + 1):
                    if 1 <= x < 11:
                        m_b[c, x, 0:8] += upper_tile
                        m_b[c, x, 8:16] += lower_tile

    @pl.loop(0, 4)
    def _(k):
        x = 2 * k + 2
        images = operate(lambda c, k: m_b[c, k], lambda k: wd[3, k], lambda k: cenw[k], x, 2)
        for i, image in enumerate(images):
            for c in range(3):
                value = m_b[c, x + i] + dinvw[x + i] * (wd[c, x + i] - image[c])
                u8[c, x + i - 2] = jnp.where(row_in_8 < 6, value[0:8], value[8:16])

    fine_u = dot(u8[...].reshape(192, 256), rz_mat[...], (((1,), (1,)), ((), ()))).reshape(3, 8, 8, 384)
    for t in range(3):
        piece = fine_u[:, :, :, 128 * t : 128 * t + 128]
        ysum[0:3, :, t, pl.ds(0, 8, stride=2), :] = piece
        ysum[0:3, :, t, pl.ds(1, 8, stride=2), :] = piece

    @pl.loop(1, 15, unroll=2)
    def _(x):
        k = x // 2
        for c in range(3):
            for t in range(3):
                lanes = slice(128 * t, 128 * t + 128)
                s_a[c, x, :, lanes] = s_b[c, x, :, lanes] + ysum[c, k, t]

    sweep(s_a, s_b, 2, 14)
    sweep(s_b, s_a, 3, 13)

    def last(k, sums):
        new = list(sums)
        for i, image in enumerate(fine(s_a)(2 * k + 4, 2)):
            x = 2 * k + i
            for c in range(3):
                p = s_a[c, x + 4, 0:8, 0:256]
                ap = image[c][0:8, 0:256]
                d = pdir[c, x]
                q = pimg[c, x]
                p_out[c, x] = p
                ap_out[c, x] = ap
                terms = (res[c, x + 4, 0:8, 0:256] * p, p * ap, p * q + d * ap, d * q)
                new = [a + b for a, b in zip(new, terms)]
        return tuple(new)

    zero = jnp.zeros((8, 256), F32)
    stores = [
        pltpu.make_async_copy(p_out, p_hbm, lsem.at[0]),
        pltpu.make_async_copy(ap_out, ap_hbm, lsem.at[1]),
    ]
    sums = lax.fori_loop(0, 4, last, (zero, zero, zero, zero))
    group = iota((1, 128), 1) // 32
    mine = jnp.zeros((1, 128), F32)
    for i, value in enumerate(sums):
        value = jnp.sum(value[:, 0:128] + value[:, 128:256], axis=0, keepdims=True)
        value = value + pltpu.roll(value, 64, 1)
        value = value + pltpu.roll(value, 32, 1)
        mine = jnp.where(group == i, value, mine)

    for peers, out, into in ((layer, dsend, drecv), (column, esend, erecv)):
        out[...] = mine
        copies = [send(out, into.at[k], d) for k, d in enumerate(peers)]
        if peers is layer:
            for copy in stores:
                copy.start()
        for copy in copies:
            copy.wait_recv()
        for k in range(len(peers)):
            mine = mine + into[k]
    inner_rz, pp, cross, qq = (
        jnp.sum(jnp.where(group == i, mine, 0.0), axis=1, keepdims=True) for i in range(4)
    )
    beta = inner_rz / prev_rz[0]
    alpha = inner_rz / (pp + beta * (cross + beta * qq))
    ab_out[...] = jnp.where(group < 2, alpha, beta)
    for copy in stores:
        copy.wait()
    for copy in started:
        copy.wait_send()


def finish(
    *refs,
):
    sources, ab_hbm, targets = refs[0:6], refs[6], refs[7:11]
    held, ab, made, sems, outs = refs[11:17], refs[17], refs[18:22], refs[22], refs[23]
    ab_load = pltpu.make_async_copy(ab_hbm, ab, sems.at[3, 0])
    ab_load.start()
    loads = [
        [pltpu.make_async_copy(src.at[c], dst.at[c], sems.at[c, i]) for i, (src, dst) in enumerate(zip(sources, held))]
        for c in range(3)
    ]
    for part in loads:
        for copy in part:
            copy.start()
    pdir, pimg, sol, res, p, ap = held
    new_sol, new_res, new_dir, new_img = made
    ab_load.wait()
    alpha = jnp.broadcast_to(ab[0:1, 0:1], (8, 256))
    beta = jnp.broadcast_to(ab[0:1, 64:65], (8, 256))
    stores = []
    for c in range(3):
        for copy in loads[c]:
            copy.wait()
        for x in range(p.shape[1]):
            direction = p[c, x] + beta * pdir[c, x]
            image = ap[c, x] + beta * pimg[c, x]
            new_dir[c, x] = direction
            new_img[c, x] = image
            new_sol[c, x] = sol[c, x] + alpha * direction
            new_res[c, x] = res[c, x] - alpha * image
        for i, (src, dst) in enumerate(zip(made, targets)):
            copy = pltpu.make_async_copy(src.at[c], dst.at[c], outs.at[c, i])
            copy.start()
            stores.append(copy)
    for copy in stores:
        copy.wait()


def solution(mesh):
    ng = tuple(mesh.shape[a] for a in AXES)

    def on_device(sol, res, pdir, pimg, prev_rz, dens, table, inverse):
        def vm(*shape):
            return pltpu.VMEM(shape, F32)

        kc = inverse.shape[3]
        n_layer, n_col = ng[0] * ng[1] - 1, ng[2] - 1
        copies = 16 + 18 + 26 + 8 + n_layer + 2 * n_col
        scratch = [
            pltpu.VMEM((8, 8, 256), jnp.int32),
            vm(3, 16, 16, 384),
            vm(18, 24, 384),
            vm(16, 16, 384), vm(16, 16, 384), vm(16, 16, 384),
            vm(3, 16, 16, 384), vm(3, 16, 16, 384),
            vm(3, 8, 8, 256), vm(3, 8, 8, 256),
            vm(2, 2, 8, 128), vm(2, 3, 3, 2, 8, 128),
            vm(4, 8, 3, 16, 128),
            vm(4, 8, 8, 256), vm(8, 8, 256), vm(8, 8, 256), vm(3, 8, 8, 256),
            vm(6, 8, 128),
            vm(2, 8, 128), vm(2, 3, 3, 8, 128),
            vm(4, 12, 16, 256), vm(12, 16, 256), vm(12, 16, 256),
            vm(3, 12, 16, 256), vm(8, 128), vm(3, 8, 8, 256),
            pltpu.VMEM((384, 256), jnp.bfloat16), pltpu.VMEM((128, 256), jnp.bfloat16),
            pltpu.VMEM((128, kc), jnp.bfloat16), vm(48, kc),
            vm(1, kc), vm(n_col, 1, kc), vm(128, kc),
            vm(1, 128), vm(3, 3, 1, 128),
            vm(1, 128), vm(n_layer, 1, 128), vm(1, 128), vm(n_col, 1, 128),
            vm(3, 8, 8, 256), vm(3, 8, 8, 256),
            pltpu.SMEM(table.shape, F32), pltpu.SMEM((1,), F32),
            pltpu.SemaphoreType.DMA((9,)),
            pltpu.SemaphoreType.DMA((copies,)),
            pltpu.SemaphoreType.DMA((copies,)),
        ]
        in_hbm = pl.BlockSpec(memory_space=pltpu.HBM)
        in_vmem = pl.BlockSpec(memory_space=pltpu.VMEM)
        field = jax.ShapeDtypeStruct(res.shape, F32)
        p, ap, ab = pl.pallas_call(
            functools.partial(kernel, ng),
            name="cg_step",
            out_shape=(field, field, jax.ShapeDtypeStruct((1, 128), F32)),
            in_specs=[in_hbm] * 7,
            out_specs=(in_hbm, in_hbm, in_vmem),
            scratch_shapes=scratch,
            compiler_params=pltpu.CompilerParams(
                collective_id=0, has_side_effects=True, vmem_limit_bytes=56 << 20
            ),
        )(res, pdir, pimg, dens, inverse, table, prev_rz.reshape(1))
        return pl.pallas_call(
            finish,
            name="cg_finish",
            out_shape=(field,) * 4,
            in_specs=[in_hbm] * 7,
            out_specs=(in_hbm,) * 4,
            scratch_shapes=[vm(*res.shape)] * 6 + [vm(1, 128)] + [vm(*res.shape)] * 4
            + [pltpu.SemaphoreType.DMA((4, 6)), pltpu.SemaphoreType.DMA((3, 4))],
            compiler_params=pltpu.CompilerParams(vmem_limit_bytes=56 << 20),
        )(pdir, pimg, sol, res, p, ap, ab)

    split = P(None, *AXES)
    return jax.shard_map(
        on_device,
        mesh=mesh,
        in_specs=(split, split, split, split, P(), P(*AXES), P(), P("gx", "gy", None, None)),
        out_specs=(split, split, split, split),
        check_vma=False,
    )
```

```python
import functools
import itertools
import math

import jax
import jax.numpy as jnp
from jax import lax
from jax.experimental import pallas as pl
from jax.experimental.pallas import tpu as pltpu
from jax.sharding import PartitionSpec as P


MESH = pl.DeviceIdType.MESH
AXES = ("gx", "gy", "gz")
F32 = jnp.float32
HIGH = lax.Precision.HIGHEST
DAMP = 0.6
UNROLL = 2
STEP = 2
EIGHTIETH = 0.0125
SMALL = (-1, 0, 1)


def iota(shape, dim):
    return lax.broadcasted_iota(jnp.int32, shape, dim)


def smooth_rows_lanes(v):
    rows, lanes = v.shape
    v = (v + v) + (pltpu.roll(v, 1, 0) + pltpu.roll(v, rows - 1, 0))
    return (v + v) + (pltpu.roll(v, 1, 1) + pltpu.roll(v, lanes - 1, 1))


def three(low, mid, high):
    return (mid + mid) + (low + high)


def operate(field, coeff, centre, at, count):
    planes = range(count + 2)
    e = [coeff(at - 1 + i) for i in planes]
    parts = [[] for _ in range(count)]
    for c in range(3):
        v = [field(c, at - 1 + i) for i in planes]
        ev = [e[i] * v[i] for i in planes]
        pair = [v[i] + v[i + 1] for i in range(count + 1)]
        epair = [ev[i] + ev[i + 1] for i in range(count + 1)]
        for i in range(count):
            plain = smooth_rows_lanes(pair[i] + pair[i + 1])
            scaled = smooth_rows_lanes(epair[i] + epair[i + 1])
            parts[i].append(centre(at + i) * v[i + 1] - EIGHTIETH * (e[i + 1] * plain + scaled))
    images = []
    for part in parts:
        shared = 0.3 * (part[0] + part[1] + part[2])
        images.append([0.7 * piece + shared for piece in part])
    return images


def centre_terms(low, mid, high):
    wide = EIGHTIETH * smooth_rows_lanes(three(low, mid, high))
    inverse = jnp.where(mid > 0.0, DAMP / (0.7 * mid + wide), 0.0)
    return 0.9 * mid + wide, inverse


def dot(a, b, dims=(((1,), (0,)), ((), ()))):
    total = None
    for part in range(3):
        piece = a.astype(jnp.bfloat16)
        term = lax.dot_general(piece, b, dims, preferred_element_type=F32)
        total = term if total is None else total + term
        if part < 2:
            a = a - piece.astype(F32)
    return total


def kernel(
    ng,
    res_hbm, dir_hbm, img_hbm, dens_hbm, inv_hbm, table_hbm, rz_hbm,
    p_hbm, ap_hbm, ab_out,
    dens, res, ewide, e16, cen, dinv, s_a, s_b, pdir, pimg,
    spack, srecv, ysum, km, cen1, dinv1, m_a, tlow,
    mpack, mrecv, wd, cenw, dinvw, m_b, m_c, u8,
    rz_mat, sel, halves, keep48, gsend, grecv, rows, wsend, wrecv,
    dsend, drecv, esend, erecv, p_out, ap_out, table, prev_rz,
    lsem, sems, recs,
):
    gx, gy, gz = (lax.axis_index(a) for a in AXES)
    me = (gx, gy, gz)

    def device(d):
        return tuple(lax.rem(me[i] + (d[i] % ng[i]), ng[i]) for i in range(3))

    def hops(d):
        return sum(min(d[i] % ng[i], -d[i] % ng[i]) for i in range(3))

    near = [d for d in itertools.product(SMALL, repeat=3) if d != (0, 0, 0)]
    near.sort(key=hops, reverse=True)
    flat = [d for d in near if d[2] == 0]
    tilted = [d for d in near if d[2] != 0]
    column = sorted(((0, 0, k) for k in range(1, ng[2])), key=hops, reverse=True)
    layer = [(i, j, 0) for i in range(ng[0]) for j in range(ng[1]) if (i, j) != (0, 0)]
    layer.sort(key=hops, reverse=True)
    partners = []
    for d in sorted(near + column + layer, key=hops, reverse=True):
        d = tuple(d[i] % ng[i] for i in range(3))
        if d not in partners:
            partners.append(d)

    loads = [
        pltpu.make_async_copy(dens_hbm, dens, lsem.at[0]),
        pltpu.make_async_copy(res_hbm, res.at[:, 4:12, 0:8, 0:256], lsem.at[1]),
        pltpu.make_async_copy(dir_hbm, pdir, lsem.at[2]),
        pltpu.make_async_copy(img_hbm, pimg, lsem.at[3]),
        pltpu.make_async_copy(rz_hbm, prev_rz, lsem.at[8]),
    ]
    table_load = pltpu.make_async_copy(table_hbm, table, lsem.at[7])
    table_load.start()
    for b in range(3):
        block = jnp.clip(gz + (b - 1), 0, ng[2] - 1)
        start = pl.multiple_of(block * 24, 8)
        loads.append(
            pltpu.make_async_copy(
                inv_hbm.at[0, 0, pl.ds(start, 24), :], rows.at[24 * b : 24 * b + 24, :], lsem.at[4 + b]
            )
        )
    for copy in loads:
        copy.start()
    barrier = pltpu.get_barrier_semaphore()
    for d in partners:
        pl.semaphore_signal(barrier, inc=1, device_id=device(d), device_id_type=MESH)
    rows[72:128, :] = jnp.zeros((56, rows.shape[1]), F32)
    table_load.wait()
    loads[0].wait()

    @pl.loop(0, 8, unroll=4)
    def _(x):
        index = dens[x]
        young = jnp.full(index.shape, table[0], F32)
        for level in range(1, table.shape[0]):
            young = jnp.where(index == level, table[level], young)
        ewide[5 + x, 8:16, 0:256] = young

    loads[1].wait()

    lane8 = iota((8, 128), 1)
    row8 = iota((8, 128), 0)
    slot8 = lane8 // 8

    def fine_tile(f, x, at):
        if f < 3:
            return res[f, 4 + x, 0:8, at : at + 128]
        return ewide[5 + x, 8:16, at : at + 128]

    for side, (at, extra) in enumerate(((0, 0), (128, 8))):
        for t in range(2):
            total = jnp.zeros((8, 128), F32)
            for k in range(2):
                for x in range(8):
                    s = k * 8 + x
                    moved = pltpu.roll(fine_tile(2 * t + k, x, at), (8 * s + extra) % 128, 1)
                    total = jnp.where(slot8 == s, moved, total)
            spack[side, t] = total

    pl.semaphore_wait(barrier, len(partners))

    started = []
    counter = [0]

    def send(src, dst, d):
        k = counter[0]
        counter[0] = k + 1
        copy = pltpu.make_async_remote_copy(
            src_ref=src, dst_ref=dst, send_sem=sems.at[k], recv_sem=recs.at[k],
            device_id=device(d), device_id_type=MESH,
        )
        copy.start()
        started.append(copy)
        return copy

    pick = {
        -1: (slice(4, 8), slice(12, 16)), 0: (slice(4, 12), slice(4, 12)), 1: (slice(8, 12), slice(0, 4)),
    }
    pick_row = {-1: (slice(0, 4), slice(8, 12)), 0: (slice(0, 8), slice(0, 8)), 1: (slice(4, 8), slice(12, 16))}
    pick_e = {
        -1: (slice(5, 10), slice(13, 18)), 0: (slice(5, 13), slice(5, 13)), 1: (slice(8, 13), slice(0, 5)),
    }
    pick_e_row = {
        -1: (slice(8, 13), slice(16, 21)), 0: (slice(8, 16), slice(8, 16)), 1: (slice(11, 16), slice(3, 8)),
    }
    main = slice(0, 256)
    round_z, round_e, round_y, round_r = [], [], [], []
    for d in tilted:
        side = 0 if d[2] < 0 else 1
        round_z.append(send(spack.at[side], srecv.at[side, 1 - d[0], 1 - d[1]], d))
    for d in flat:
        src = ewide.at[pick_e[d[0]][0], pick_e_row[d[1]][0], main]
        dst = ewide.at[pick_e[d[0]][1], pick_e_row[d[1]][1], main]
        round_e.append(send(src, dst, d))
    for d in reversed(flat):
        src = res.at[:, pick[d[0]][0], pick_row[d[1]][0], main]
        dst = res.at[:, pick[d[0]][1], pick_row[d[1]][1], main]
        (round_y if d[0] == 0 else round_r).append(send(src, dst, d))

    lane_of = iota((384, 256), 0)
    target = jnp.where(lane_of < 320, lane_of // 2, lane_of // 2 + 64)
    rz_mat[...] = jnp.where(iota((384, 256), 1) == target, 1.0, 0.0).astype(jnp.bfloat16)
    place = iota((128, 384), 1) - 24 * gz
    halves[...] = jnp.where((place & 1) == iota((128, 384), 0) // 64, 1.0 / 16.0, 0.0).astype(jnp.bfloat16)
    place = iota((48, 384), 1) - 24 * gz
    row48 = iota((48, 384), 0)
    keep = (place >= 0) & (place < 24) & ((place // 4) == (row48 // 8))
    keep = keep & ((row48 % 8) // 2 == (place // 2) % 2) & (row48 % 8 < 4)
    keep48[...] = jnp.where(keep, 1.0, 0.0)

    col = iota((128, 256), 0)
    quarter = iota((128, 256), 1) // 64
    code = 2 * (col // 24) + (col % 2)
    sel[...] = jnp.where(code == jnp.where(quarter == 3, 1, quarter + 2), 1.0, 0.0).astype(jnp.bfloat16)

    for copy in round_z:
        copy.wait_recv()

    def rim(right, left, s):
        to_right = pltpu.roll(right, (-8 * s) % 128, 1)
        to_left = pltpu.roll(left, (-8 * s - 8) % 128, 1)
        return jnp.where(lane8 < 64, to_right, to_left)

    rim_lanes = slice(256, 384)
    for ox, first, count, base in ((-1, 4, 4, 0), (0, 0, 8, 4), (1, 0, 4, 12)):
        for t in range(2):
            tiles = [srecv[side, ox + 1, 1, t] for side in range(2)]
            mixed = [
                jnp.where(row8 < 4, srecv[side, ox + 1, 2, t], srecv[side, ox + 1, 0, t]) for side in range(2)
            ]

            for i in range(count):
                for k in range(2):
                    if 2 * t + k < 3:
                        s = k * 8 + first + i
                        res[2 * t + k, base + i, 0:8, rim_lanes] = rim(tiles[0], tiles[1], s)
                        res[2 * t + k, base + i, 8:16, rim_lanes] = rim(mixed[0], mixed[1], s)

    for ox, first, count, base in ((-1, 3, 5, 0), (0, 0, 8, 5), (1, 0, 5, 13)):
        tiles = [[srecv[side, ox + 1, oy, 1] for side in range(2)] for oy in range(3)]

        for i in range(count):
            for oy in range(3):
                ewide[base + i, 8 * oy : 8 * oy + 8, rim_lanes] = rim(tiles[oy][0], tiles[oy][1], 8 + first + i)

    row24 = iota((24, 384), 0)
    lane24 = iota((24, 384), 1)
    y_at = gy * 8 + row24 - 8
    z_at = gz * 256 + jnp.where(lane24 < 320, lane24, lane24 - 384)
    inside = (y_at >= 0) & (y_at < 8 * ng[1]) & (z_at >= 0) & (z_at < 256 * ng[2])
    inside = inside & ((lane24 < 264) | (lane24 >= 376)) & (row24 >= 3) & (row24 < 21)
    inside = jnp.where(inside, 1, 0)
    for copy in round_e:
        copy.wait_recv()
    upper = iota((8, 384), 0) < 4

    def fold(value):
        return jnp.concatenate([value[8:16], jnp.where(upper, value[16:24], value[0:8])], axis=0)

    def masked(x):
        x_at = gx * 8 + x - 5
        x_in = jnp.where((x_at >= 0) & (x_at < 8 * ng[0]), 1, 0)
        return jnp.where(inside * x_in > 0, ewide[x], 0.0)

    @pl.loop(0, 16, unroll=2)
    def _(x):
        low, mid, high = masked(x), masked(x + 1), masked(x + 2)
        wide = three(low, mid, high)
        wide = fold((wide + wide) + (pltpu.roll(wide, 1, 0) + pltpu.roll(wide, 23, 0)))
        wide = EIGHTIETH * ((wide + wide) + (pltpu.roll(wide, 1, 1) + pltpu.roll(wide, 383, 1)))
        mid = fold(mid)
        inverse = jnp.where(mid > 0.0, DAMP / (0.7 * mid + wide), 0.0)
        e16[x] = mid
        cen[x] = 0.9 * mid + wide
        dinv[x] = inverse

    def begin(start, stop):
        @pl.loop(start, stop, unroll=4)
        def _(x):
            for c in range(3):
                s_a[c, x] = dinv[x] * res[c, x]

    for copy in round_y:
        copy.wait_recv()
    begin(4, 12)

    def fine(ref):
        return functools.partial(
            operate, lambda c, x: ref[c, x], lambda x: e16[x], lambda x: cen[x]
        )

    def sweep(source, out, start, stop, count=STEP):
        assert (stop - start) % count == 0

        @pl.loop(0, (stop - start) // count, unroll=UNROLL)
        def _(k):
            x = start + count * k
            for i, image in enumerate(fine(source)(x, count)):
                for c in range(3):
                    out[c, x + i] = source[c, x + i] + dinv[x + i] * (res[c, x + i] - image[c])

    sweep(s_a, s_b, 5, 11, 2)
    for copy in round_r:
        copy.wait_recv()
    begin(0, 4)
    begin(12, 16)
    sweep(s_a, s_b, 1, 5, 2)
    sweep(s_a, s_b, 11, 15, 2)

    def put_tiles(ref, f, k, value):
        for t in range(3):
            ref[f, k, t] = value[:, 128 * t : 128 * t + 128]

    @pl.loop(0, 6)
    def _(k):
        x = 2 * k + 2
        first, second = fine(s_b)(x, 2)
        for c in range(3):
            both = (res[c, x] - first[c]) + (res[c, x + 1] - second[c])
            put_tiles(ysum, c, k + 1, both + pltpu.roll(both, 15, 0))

    @pl.loop(0, 8, unroll=4)
    def _(k):
        both = e16[2 * k] + e16[2 * k + 1]
        put_tiles(ysum, 3, k, both + pltpu.roll(both, 15, 0))

    for c in range(3):
        for k in (0, 7):
            ysum[c, k] = jnp.zeros((3, 16, 128), F32)

    total = None
    for t in range(3):
        left = ysum[:, :, t, pl.ds(0, 8, stride=2), :].reshape(256, 128)
        part = dot(left, rz_mat[128 * t : 128 * t + 128, :])
        total = part if total is None else total + part
    total = total.reshape(4, 8, 8, 256)
    km[0:3] = 0.5 * total[0:3]
    km[3] = 0.125 * total[3]

    @pl.loop(1, 7, unroll=3)
    def _(k):
        own, inverse = centre_terms(km[3, k - 1], km[3, k], km[3, k + 1])
        cen1[k] = own
        dinv1[k] = inverse
        for c in range(3):
            m_a[c, k] = inverse * km[c, k]

    @pl.loop(0, 2)
    def _(b):
        x = 2 * b + 2
        apply = functools.partial(
            operate, lambda c, k: m_a[c, k], lambda k: km[3, k], lambda k: cen1[k]
        )
        first, second = apply(x, 2)
        for c in range(3):
            both = (km[c, x] - first[c]) + (km[c, x + 1] - second[c])
            tlow[2 * c + b] = both[:, 0:128]

    spread = dot(tlow[...].reshape(48, 128), halves[...])
    own_g = jnp.sum(jnp.where(keep48[...] > 0.0, spread, 0.0), axis=0, keepdims=True)
    gsend[...] = own_g
    round_b = [send(gsend, grecv.at[k], d) for k, d in enumerate(column)]

    low = iota((8, 128), 0) < 4
    for side, (at, extra) in enumerate(((0, 0), (0, 8))):
        total = jnp.zeros((8, 128), F32)
        for f in range(4):
            for x in range(4):
                s = 4 * f + x
                moved = pltpu.roll(km[f, 2 + x, :, 0:128], (8 * s + extra) % 128, 1)
                total = jnp.where(slot8 == s, moved, total)
        mpack[side] = jnp.where(low, total, pltpu.roll(total, 4, 0))
    round_c = []
    mid_x = {-1: slice(8, 12), 0: slice(4, 8), 1: slice(0, 4)}
    mid_row = {-1: slice(4, 8), 0: slice(0, 4), 1: slice(12, 16)}
    block = km.at[:, 2:6, 0:4, 0:128]
    for d in flat:
        round_c.append(send(block, wd.at[:, mid_x[d[0]], mid_row[d[1]], 0:128], d))
    for d in tilted:
        side = 0 if d[2] < 0 else 1
        round_c.append(send(mpack.at[side], mrecv.at[side, 1 - d[0], 1 - d[1]], d))
    for f in range(4):
        wd[f, 4:8, 0:4, 0:128] = km[f, 2:6, 0:4, 0:128]
        wd[f, :, 8:12, 0:128] = jnp.zeros((12, 4, 128), F32)
    for copy in loads[2:]:
        copy.wait()
    for copy in round_b:
        copy.wait_recv()
    g = own_g
    for k in range(len(column)):
        g = g + grecv[k]
    g = jnp.broadcast_to(g, (8, g.shape[1]))
    w = lax.dot_general(
        g, rows[...], (((1,), (1,)), ((), ())), precision=HIGH, preferred_element_type=F32
    )
    wsend[...] = w[0:1, :]
    round_d = [send(wsend, wrecv.at[1 - d[0], 1 - d[1]], d) for d in flat]

    for copy in round_c:
        copy.wait_recv()
    for ox in range(3):
        near_y = [jnp.where(low, mrecv[side, ox, 1], mrecv[side, ox, 2]) for side in range(2)]
        far_y = [mrecv[side, ox, 0] for side in range(2)]
        for f in range(4):
            for x in range(4):
                s = 4 * f + x
                wd[f, 4 * ox + x, 0:8, 128:256] = rim(near_y[0], near_y[1], s)
                wd[f, 4 * ox + x, 8:16, 128:256] = rim(far_y[0], far_y[1], s)
    row16 = iota((16, 256), 0)
    lane16 = iota((16, 256), 1)
    y_at = gy * 4 + jnp.where(row16 < 8, row16, row16 - 16)
    z_at = gz * 128 + jnp.where(lane16 < 192, lane16, lane16 - 256)
    inside = (y_at >= 0) & (y_at < 4 * ng[1]) & (z_at >= 0) & (z_at < 128 * ng[2])
    inside = inside & ((row16 < 8) | (row16 >= 12)) & ((lane16 < 136) | (lane16 >= 248))
    inside = jnp.where(inside, 1, 0)

    @pl.loop(0, 12, unroll=4)
    def _(x):
        x_at = gx * 4 + x - 4
        x_in = jnp.where((x_at >= 0) & (x_at < 4 * ng[0]), 1, 0)
        wd[3, x] = jnp.where(inside * x_in > 0, wd[3, x], 0.0)

    @pl.loop(1, 11, unroll=2)
    def _(x):
        own, inverse = centre_terms(wd[3, x - 1], wd[3, x], wd[3, x + 1])
        cenw[x] = own
        dinvw[x] = inverse
        for c in range(3):
            m_b[c, x] = inverse * wd[c, x]

    col = iota((16, 128), 1)
    blk = col // 24
    keep = (col < 72) & ((col % 24) // 2 == iota((16, 128), 0))
    keep = keep & ((blk != 0) | (gz > 0)) & ((blk != 2) | (gz < ng[2] - 1))
    for copy in round_d:
        copy.wait_recv()
    picked = []
    for ox in range(3):
        for oy in range(3):
            x_at, y_at = gx + (ox - 1), gy + (oy - 1)
            known = (x_at >= 0) & (x_at < ng[0]) & (y_at >= 0) & (y_at < ng[1])
            line = wsend[...] if (ox, oy) == (1, 1) else wrecv[ox, oy]
            line = jnp.broadcast_to(line * jnp.where(known, 1.0, 0.0), (16, 128))
            picked.append(jnp.where(keep, line, 0.0))
    blocks = dot(jnp.concatenate(picked, axis=0), sel[...])

    row_in_8 = iota((8, 256), 0)
    for ox in range(3):
        values = [blocks[16 * (3 * ox + oy) : 16 * (3 * ox + oy) + 16] for oy in range(3)]
        for xb in range(2):
            for c in range(3):
                r = 4 * c + 2 * xb

                def line(oy, k, r=r, values=values):
                    return jnp.broadcast_to(values[oy][r + k : r + k + 1, :], (8, 256))

                upper_tile = jnp.where(
                    row_in_8 < 4,
                    jnp.where(row_in_8 < 2, line(1, 0), line(1, 1)),
                    jnp.where(row_in_8 < 6, line(2, 0), line(2, 1)),
                )
                lower_tile = jnp.where(row_in_8 < 6, line(0, 0), line(0, 1))
                for x in (4 * ox + 2 * xb, 4 * ox + 2 * xb + 1):
                    if 1 <= x < 11:
                        m_b[c, x, 0:8] += upper_tile
                        m_b[c, x, 8:16] += lower_tile

    @pl.loop(0, 4)
    def _(k):
        x = 2 * k + 2
        images = operate(lambda c, k: m_b[c, k], lambda k: wd[3, k], lambda k: cenw[k], x, 2)
        for i, image in enumerate(images):
            for c in range(3):
                value = m_b[c, x + i] + dinvw[x + i] * (wd[c, x + i] - image[c])
                u8[c, x + i - 2] = jnp.where(row_in_8 < 6, value[0:8], value[8:16])

    fine_u = dot(u8[...].reshape(192, 256), rz_mat[...], (((1,), (1,)), ((), ()))).reshape(3, 8, 8, 384)
    for t in range(3):
        piece = fine_u[:, :, :, 128 * t : 128 * t + 128]
        ysum[0:3, :, t, pl.ds(0, 8, stride=2), :] = piece
        ysum[0:3, :, t, pl.ds(1, 8, stride=2), :] = piece

    @pl.loop(1, 15, unroll=2)
    def _(x):
        k = x // 2
        for c in range(3):
            for t in range(3):
                lanes = slice(128 * t, 128 * t + 128)
                s_a[c, x, :, lanes] = s_b[c, x, :, lanes] + ysum[c, k, t]

    sweep(s_a, s_b, 2, 14)
    sweep(s_b, s_a, 3, 13)

    def last(k, sums):
        new = list(sums)
        for i, image in enumerate(fine(s_a)(2 * k + 4, 2)):
            x = 2 * k + i
            for c in range(3):
                p = s_a[c, x + 4, 0:8, 0:256]
                ap = image[c][0:8, 0:256]
                d = pdir[c, x]
                q = pimg[c, x]
                p_out[c, x] = p
                ap_out[c, x] = ap
                terms = (res[c, x + 4, 0:8, 0:256] * p, p * ap, p * q + d * ap, d * q)
                new = [a + b for a, b in zip(new, terms)]
        return tuple(new)

    zero = jnp.zeros((8, 256), F32)
    stores = [
        pltpu.make_async_copy(p_out, p_hbm, lsem.at[0]),
        pltpu.make_async_copy(ap_out, ap_hbm, lsem.at[1]),
    ]
    sums = lax.fori_loop(0, 4, last, (zero, zero, zero, zero))
    group = iota((1, 128), 1) // 32
    mine = jnp.zeros((1, 128), F32)
    for i, value in enumerate(sums):
        value = jnp.sum(value[:, 0:128] + value[:, 128:256], axis=0, keepdims=True)
        value = value + pltpu.roll(value, 64, 1)
        value = value + pltpu.roll(value, 32, 1)
        mine = jnp.where(group == i, value, mine)

    pending = list(started)
    for peers, out, into in ((layer, dsend, drecv), (column, esend, erecv)):
        out[...] = mine
        copies = [send(out, into.at[k], d) for k, d in enumerate(peers)]
        if peers is layer:
            for copy in stores:
                copy.start()
        else:
            for copy in stores:
                copy.wait()
        for copy in pending:
            copy.wait_send()
        pending = copies
        for copy in copies:
            copy.wait_recv()
        for k in range(len(peers)):
            mine = mine + into[k]
    inner_rz, pp, cross, qq = (
        jnp.sum(jnp.where(group == i, mine, 0.0), axis=1, keepdims=True) for i in range(4)
    )
    beta = inner_rz / prev_rz[0]
    alpha = inner_rz / (pp + beta * (cross + beta * qq))
    ab_out[...] = jnp.where(group < 2, alpha, beta)
    for copy in pending:
        copy.wait_send()


def finish(
    *refs,
):
    sources, ab_hbm, targets = refs[0:6], refs[6], refs[7:11]
    held, ab, made, sems, outs = refs[11:17], refs[17], refs[18:22], refs[22], refs[23]
    ab_load = pltpu.make_async_copy(ab_hbm, ab, sems.at[3, 0])
    ab_load.start()
    loads = [
        [pltpu.make_async_copy(src.at[c], dst.at[c], sems.at[c, i]) for i, (src, dst) in enumerate(zip(sources, held))]
        for c in range(3)
    ]
    for part in loads:
        for copy in part:
            copy.start()
    pdir, pimg, sol, res, p, ap = held
    new_sol, new_res, new_dir, new_img = made
    ab_load.wait()
    alpha = jnp.broadcast_to(ab[0:1, 0:1], (8, 256))
    beta = jnp.broadcast_to(ab[0:1, 64:65], (8, 256))
    stores = []
    for c in range(3):
        for copy in loads[c]:
            copy.wait()
        for x in range(p.shape[1]):
            direction = p[c, x] + beta * pdir[c, x]
            image = ap[c, x] + beta * pimg[c, x]
            new_dir[c, x] = direction
            new_img[c, x] = image
            new_sol[c, x] = sol[c, x] + alpha * direction
            new_res[c, x] = res[c, x] - alpha * image
        for i, (src, dst) in enumerate(zip(made, targets)):
            copy = pltpu.make_async_copy(src.at[c], dst.at[c], outs.at[c, i])
            copy.start()
            stores.append(copy)
    for copy in stores:
        copy.wait()


def solution(mesh):
    ng = tuple(mesh.shape[a] for a in AXES)

    def on_device(sol, res, pdir, pimg, prev_rz, dens, table, inverse):
        def vm(*shape):
            return pltpu.VMEM(shape, F32)

        kc = inverse.shape[3]
        n_layer, n_col = ng[0] * ng[1] - 1, ng[2] - 1
        copies = 16 + 18 + 26 + 8 + n_layer + 2 * n_col
        scratch = [
            pltpu.VMEM((8, 8, 256), jnp.int32),
            vm(3, 16, 16, 384),
            vm(18, 24, 384),
            vm(16, 16, 384), vm(16, 16, 384), vm(16, 16, 384),
            vm(3, 16, 16, 384), vm(3, 16, 16, 384),
            vm(3, 8, 8, 256), vm(3, 8, 8, 256),
            vm(2, 2, 8, 128), vm(2, 3, 3, 2, 8, 128),
            vm(4, 8, 3, 16, 128),
            vm(4, 8, 8, 256), vm(8, 8, 256), vm(8, 8, 256), vm(3, 8, 8, 256),
            vm(6, 8, 128),
            vm(2, 8, 128), vm(2, 3, 3, 8, 128),
            vm(4, 12, 16, 256), vm(12, 16, 256), vm(12, 16, 256),
            vm(3, 12, 16, 256), vm(8, 128), vm(3, 8, 8, 256),
            pltpu.VMEM((384, 256), jnp.bfloat16), pltpu.VMEM((128, 256), jnp.bfloat16),
            pltpu.VMEM((128, kc), jnp.bfloat16), vm(48, kc),
            vm(1, kc), vm(n_col, 1, kc), vm(128, kc),
            vm(1, 128), vm(3, 3, 1, 128),
            vm(1, 128), vm(n_layer, 1, 128), vm(1, 128), vm(n_col, 1, 128),
            vm(3, 8, 8, 256), vm(3, 8, 8, 256),
            pltpu.SMEM(table.shape, F32), pltpu.SMEM((1,), F32),
            pltpu.SemaphoreType.DMA((9,)),
            pltpu.SemaphoreType.DMA((copies,)),
            pltpu.SemaphoreType.DMA((copies,)),
        ]
        in_hbm = pl.BlockSpec(memory_space=pltpu.HBM)
        in_vmem = pl.BlockSpec(memory_space=pltpu.VMEM)
        field = jax.ShapeDtypeStruct(res.shape, F32)
        p, ap, ab = pl.pallas_call(
            functools.partial(kernel, ng),
            name="cg_step",
            out_shape=(field, field, jax.ShapeDtypeStruct((1, 128), F32)),
            in_specs=[in_hbm] * 7,
            out_specs=(in_hbm, in_hbm, in_vmem),
            scratch_shapes=scratch,
            compiler_params=pltpu.CompilerParams(
                collective_id=0, has_side_effects=True, vmem_limit_bytes=56 << 20
            ),
        )(res, pdir, pimg, dens, inverse, table, prev_rz.reshape(1))
        return pl.pallas_call(
            finish,
            name="cg_finish",
            out_shape=(field,) * 4,
            in_specs=[in_hbm] * 7,
            out_specs=(in_hbm,) * 4,
            scratch_shapes=[vm(*res.shape)] * 6 + [vm(1, 128)] + [vm(*res.shape)] * 4
            + [pltpu.SemaphoreType.DMA((4, 6)), pltpu.SemaphoreType.DMA((3, 4))],
            compiler_params=pltpu.CompilerParams(vmem_limit_bytes=56 << 20),
        )(pdir, pimg, sol, res, p, ap, ab)

    split = P(None, *AXES)
    return jax.shard_map(
        on_device,
        mesh=mesh,
        in_specs=(split, split, split, split, P(), P(*AXES), P(), P("gx", "gy", None, None)),
        out_specs=(split, split, split, split),
        check_vma=False,
    )
```

```python
import functools
import itertools
import math

import jax
import jax.numpy as jnp
from jax import lax
from jax.experimental import pallas as pl
from jax.experimental.pallas import tpu as pltpu
from jax.sharding import PartitionSpec as P


MESH = pl.DeviceIdType.MESH
AXES = ("gx", "gy", "gz")
F32 = jnp.float32
HIGH = lax.Precision.HIGHEST
DAMP = 0.6
UNROLL = 2
STEP = 2
HELD = 300
EIGHTIETH = 0.0125
SMALL = (-1, 0, 1)


def iota(shape, dim):
    return lax.broadcasted_iota(jnp.int32, shape, dim)


def smooth_rows_lanes(v):
    rows, lanes = v.shape
    v = (v + v) + (pltpu.roll(v, 1, 0) + pltpu.roll(v, rows - 1, 0))
    return (v + v) + (pltpu.roll(v, 1, 1) + pltpu.roll(v, lanes - 1, 1))


def three(low, mid, high):
    return (mid + mid) + (low + high)


def operate(field, coeff, centre, at, count):
    planes = range(count + 2)
    e = [coeff(at - 1 + i) for i in planes]
    parts = [[] for _ in range(count)]
    for c in range(3):
        v = [field(c, at - 1 + i) for i in planes]
        ev = [e[i] * v[i] for i in planes]
        pair = [v[i] + v[i + 1] for i in range(count + 1)]
        epair = [ev[i] + ev[i + 1] for i in range(count + 1)]
        for i in range(count):
            plain = smooth_rows_lanes(pair[i] + pair[i + 1])
            scaled = smooth_rows_lanes(epair[i] + epair[i + 1])
            parts[i].append(centre(at + i) * v[i + 1] - EIGHTIETH * (e[i + 1] * plain + scaled))
    images = []
    for part in parts:
        shared = 0.3 * (part[0] + part[1] + part[2])
        images.append([0.7 * piece + shared for piece in part])
    return images


def centre_terms(low, mid, high):
    wide = EIGHTIETH * smooth_rows_lanes(three(low, mid, high))
    inverse = jnp.where(mid > 0.0, DAMP / (0.7 * mid + wide), 0.0)
    return 0.9 * mid + wide, inverse


def dot(a, b, dims=(((1,), (0,)), ((), ()))):
    total = None
    for part in range(3):
        piece = a.astype(jnp.bfloat16)
        term = lax.dot_general(piece, b, dims, preferred_element_type=F32)
        total = term if total is None else total + term
        if part < 2:
            a = a - piece.astype(F32)
    return total


def kernel(
    ng,
    res_hbm, dir_hbm, img_hbm, dens_hbm, inv_hbm, table_hbm, rz_hbm,
    held_hbm,
    dens, res, ewide, e16, cen, dinv, s_a, s_b, pdir, pimg,
    spack, srecv, ysum, km, cen1, dinv1, m_a, tlow,
    mpack, mrecv, wd, cenw, dinvw, m_b, m_c, u8,
    rz_mat, sel, halves, keep48, gsend, grecv, rows, wsend, wrecv,
    dsend, drecv, esend, erecv, p_out, ap_out, ab_out, table, prev_rz,
    lsem, sems, recs,
):
    gx, gy, gz = (lax.axis_index(a) for a in AXES)
    me = (gx, gy, gz)

    def device(d):
        return tuple(lax.rem(me[i] + (d[i] % ng[i]), ng[i]) for i in range(3))

    def hops(d):
        return sum(min(d[i] % ng[i], -d[i] % ng[i]) for i in range(3))

    near = [d for d in itertools.product(SMALL, repeat=3) if d != (0, 0, 0)]
    near.sort(key=hops, reverse=True)
    flat = [d for d in near if d[2] == 0]
    tilted = [d for d in near if d[2] != 0]
    column = sorted(((0, 0, k) for k in range(1, ng[2])), key=hops, reverse=True)
    layer = [(i, j, 0) for i in range(ng[0]) for j in range(ng[1]) if (i, j) != (0, 0)]
    layer.sort(key=hops, reverse=True)
    partners = []
    for d in sorted(near + column + layer, key=hops, reverse=True):
        d = tuple(d[i] % ng[i] for i in range(3))
        if d not in partners:
            partners.append(d)

    loads = [
        pltpu.make_async_copy(dens_hbm, dens, lsem.at[0]),
        pltpu.make_async_copy(res_hbm, res.at[:, 4:12, 0:8, 0:256], lsem.at[1]),
        pltpu.make_async_copy(dir_hbm, pdir, lsem.at[2]),
        pltpu.make_async_copy(img_hbm, pimg, lsem.at[3]),
        pltpu.make_async_copy(rz_hbm, prev_rz, lsem.at[8]),
    ]
    table_load = pltpu.make_async_copy(table_hbm, table, lsem.at[7])
    table_load.start()
    for b in range(3):
        block = jnp.clip(gz + (b - 1), 0, ng[2] - 1)
        start = pl.multiple_of(block * 24, 8)
        loads.append(
            pltpu.make_async_copy(
                inv_hbm.at[0, 0, pl.ds(start, 24), :], rows.at[24 * b : 24 * b + 24, :], lsem.at[4 + b]
            )
        )
    for copy in loads:
        copy.start()
    barrier = pltpu.get_barrier_semaphore()
    for d in partners:
        pl.semaphore_signal(barrier, inc=1, device_id=device(d), device_id_type=MESH)
    rows[72:128, :] = jnp.zeros((56, rows.shape[1]), F32)
    table_load.wait()
    loads[0].wait()

    @pl.loop(0, 8, unroll=4)
    def _(x):
        index = dens[x]
        young = jnp.full(index.shape, table[0], F32)
        for level in range(1, table.shape[0]):
            young = jnp.where(index == level, table[level], young)
        ewide[5 + x, 8:16, 0:256] = young

    loads[1].wait()

    lane8 = iota((8, 128), 1)
    row8 = iota((8, 128), 0)
    slot8 = lane8 // 8

    def fine_tile(f, x, at):
        if f < 3:
            return res[f, 4 + x, 0:8, at : at + 128]
        return ewide[5 + x, 8:16, at : at + 128]

    for side, (at, extra) in enumerate(((0, 0), (128, 8))):
        for t in range(2):
            total = jnp.zeros((8, 128), F32)
            for k in range(2):
                for x in range(8):
                    s = k * 8 + x
                    moved = pltpu.roll(fine_tile(2 * t + k, x, at), (8 * s + extra) % 128, 1)
                    total = jnp.where(slot8 == s, moved, total)
            spack[side, t] = total

    pl.semaphore_wait(barrier, len(partners))

    started = []
    counter = [0]

    def send(src, dst, d):
        k = counter[0]
        counter[0] = k + 1
        copy = pltpu.make_async_remote_copy(
            src_ref=src, dst_ref=dst, send_sem=sems.at[k], recv_sem=recs.at[k],
            device_id=device(d), device_id_type=MESH,
        )
        copy.start()
        started.append(copy)
        return copy

    pick = {
        -1: (slice(4, 8), slice(12, 16)), 0: (slice(4, 12), slice(4, 12)), 1: (slice(8, 12), slice(0, 4)),
    }
    pick_row = {-1: (slice(0, 4), slice(8, 12)), 0: (slice(0, 8), slice(0, 8)), 1: (slice(4, 8), slice(12, 16))}
    pick_e = {
        -1: (slice(5, 10), slice(13, 18)), 0: (slice(5, 13), slice(5, 13)), 1: (slice(8, 13), slice(0, 5)),
    }
    pick_e_row = {
        -1: (slice(8, 13), slice(16, 21)), 0: (slice(8, 16), slice(8, 16)), 1: (slice(11, 16), slice(3, 8)),
    }
    main = slice(0, 256)
    round_z, round_e, round_y, round_r = [], [], [], []
    for d in tilted[::-1]:
        side = 0 if d[2] < 0 else 1
        round_z.append(send(spack.at[side], srecv.at[side, 1 - d[0], 1 - d[1]], d))
    for d in flat:
        src = ewide.at[pick_e[d[0]][0], pick_e_row[d[1]][0], main]
        dst = ewide.at[pick_e[d[0]][1], pick_e_row[d[1]][1], main]
        round_e.append(send(src, dst, d))
    for d in reversed(flat):
        src = res.at[:, pick[d[0]][0], pick_row[d[1]][0], main]
        dst = res.at[:, pick[d[0]][1], pick_row[d[1]][1], main]
        (round_y if d[0] == 0 else round_r).append(send(src, dst, d))

    lane_of = iota((384, 256), 0)
    target = jnp.where(lane_of < 320, lane_of // 2, lane_of // 2 + 64)
    rz_mat[...] = jnp.where(iota((384, 256), 1) == target, 1.0, 0.0).astype(jnp.bfloat16)
    place = iota((128, 384), 1) - 24 * gz
    halves[...] = jnp.where((place & 1) == iota((128, 384), 0) // 64, 1.0 / 16.0, 0.0).astype(jnp.bfloat16)
    place = iota((48, 384), 1) - 24 * gz
    row48 = iota((48, 384), 0)
    keep = (place >= 0) & (place < 24) & ((place // 4) == (row48 // 8))
    keep = keep & ((row48 % 8) // 2 == (place // 2) % 2) & (row48 % 8 < 4)
    keep48[...] = jnp.where(keep, 1.0, 0.0)

    col = iota((128, 256), 0)
    quarter = iota((128, 256), 1) // 64
    code = 2 * (col // 24) + (col % 2)
    sel[...] = jnp.where(code == jnp.where(quarter == 3, 1, quarter + 2), 1.0, 0.0).astype(jnp.bfloat16)

    for copy in round_z:
        copy.wait_recv()

    def rim(right, left, s):
        to_right = pltpu.roll(right, (-8 * s) % 128, 1)
        to_left = pltpu.roll(left, (-8 * s - 8) % 128, 1)
        return jnp.where(lane8 < 64, to_right, to_left)

    rim_lanes = slice(256, 384)
    for ox, first, count, base in ((-1, 4, 4, 0), (0, 0, 8, 4), (1, 0, 4, 12)):
        for t in range(2):
            tiles = [srecv[side, ox + 1, 1, t] for side in range(2)]
            mixed = [
                jnp.where(row8 < 4, srecv[side, ox + 1, 2, t], srecv[side, ox + 1, 0, t]) for side in range(2)
            ]

            for i in range(count):
                for k in range(2):
                    if 2 * t + k < 3:
                        s = k * 8 + first + i
                        res[2 * t + k, base + i, 0:8, rim_lanes] = rim(tiles[0], tiles[1], s)
                        res[2 * t + k, base + i, 8:16, rim_lanes] = rim(mixed[0], mixed[1], s)

    for ox, first, count, base in ((-1, 3, 5, 0), (0, 0, 8, 5), (1, 0, 5, 13)):
        tiles = [[srecv[side, ox + 1, oy, 1] for side in range(2)] for oy in range(3)]

        for i in range(count):
            for oy in range(3):
                ewide[base + i, 8 * oy : 8 * oy + 8, rim_lanes] = rim(tiles[oy][0], tiles[oy][1], 8 + first + i)

    row24 = iota((24, 384), 0)
    lane24 = iota((24, 384), 1)
    y_at = gy * 8 + row24 - 8
    z_at = gz * 256 + jnp.where(lane24 < 320, lane24, lane24 - 384)
    inside = (y_at >= 0) & (y_at < 8 * ng[1]) & (z_at >= 0) & (z_at < 256 * ng[2])
    inside = inside & ((lane24 < 264) | (lane24 >= 376)) & (row24 >= 3) & (row24 < 21)
    inside = jnp.where(inside, 1, 0)
    for copy in round_e:
        copy.wait_recv()
    upper = iota((8, 384), 0) < 4

    def fold(value):
        return jnp.concatenate([value[8:16], jnp.where(upper, value[16:24], value[0:8])], axis=0)

    def masked(x):
        x_at = gx * 8 + x - 5
        x_in = jnp.where((x_at >= 0) & (x_at < 8 * ng[0]), 1, 0)
        return jnp.where(inside * x_in > 0, ewide[x], 0.0)

    @pl.loop(0, 16, unroll=2)
    def _(x):
        low, mid, high = masked(x), masked(x + 1), masked(x + 2)
        wide = three(low, mid, high)
        wide = fold((wide + wide) + (pltpu.roll(wide, 1, 0) + pltpu.roll(wide, 23, 0)))
        wide = EIGHTIETH * ((wide + wide) + (pltpu.roll(wide, 1, 1) + pltpu.roll(wide, 383, 1)))
        mid = fold(mid)
        inverse = jnp.where(mid > 0.0, DAMP / (0.7 * mid + wide), 0.0)
        e16[x] = mid
        cen[x] = 0.9 * mid + wide
        dinv[x] = inverse

    def begin(start, stop):
        @pl.loop(start, stop, unroll=4)
        def _(x):
            for c in range(3):
                s_a[c, x] = dinv[x] * res[c, x]

    for copy in round_y:
        copy.wait_recv()
    begin(4, 12)

    def fine(ref):
        return functools.partial(
            operate, lambda c, x: ref[c, x], lambda x: e16[x], lambda x: cen[x]
        )

    def sweep(source, out, start, stop, count=STEP):
        assert (stop - start) % count == 0

        @pl.loop(0, (stop - start) // count, unroll=UNROLL)
        def _(k):
            x = start + count * k
            for i, image in enumerate(fine(source)(x, count)):
                for c in range(3):
                    out[c, x + i] = source[c, x + i] + dinv[x + i] * (res[c, x + i] - image[c])

    sweep(s_a, s_b, 5, 11, 2)
    for copy in round_r:
        copy.wait_recv()
    begin(0, 4)
    begin(12, 16)
    sweep(s_a, s_b, 1, 5, 2)
    sweep(s_a, s_b, 11, 15, 2)

    def put_tiles(ref, f, k, value):
        for t in range(3):
            ref[f, k, t] = value[:, 128 * t : 128 * t + 128]

    @pl.loop(0, 6)
    def _(k):
        x = 2 * k + 2
        first, second = fine(s_b)(x, 2)
        for c in range(3):
            both = (res[c, x] - first[c]) + (res[c, x + 1] - second[c])
            put_tiles(ysum, c, k + 1, both + pltpu.roll(both, 15, 0))

    @pl.loop(0, 8, unroll=4)
    def _(k):
        both = e16[2 * k] + e16[2 * k + 1]
        put_tiles(ysum, 3, k, both + pltpu.roll(both, 15, 0))

    for c in range(3):
        for k in (0, 7):
            ysum[c, k] = jnp.zeros((3, 16, 128), F32)

    total = None
    for t in range(3):
        left = ysum[:, :, t, pl.ds(0, 8, stride=2), :].reshape(256, 128)
        part = dot(left, rz_mat[128 * t : 128 * t + 128, :])
        total = part if total is None else total + part
    total = total.reshape(4, 8, 8, 256)
    km[0:3] = 0.5 * total[0:3]
    km[3] = 0.125 * total[3]

    @pl.loop(1, 7, unroll=3)
    def _(k):
        own, inverse = centre_terms(km[3, k - 1], km[3, k], km[3, k + 1])
        cen1[k] = own
        dinv1[k] = inverse
        for c in range(3):
            m_a[c, k] = inverse * km[c, k]

    @pl.loop(0, 2)
    def _(b):
        x = 2 * b + 2
        apply = functools.partial(
            operate, lambda c, k: m_a[c, k], lambda k: km[3, k], lambda k: cen1[k]
        )
        first, second = apply(x, 2)
        for c in range(3):
            both = (km[c, x] - first[c]) + (km[c, x + 1] - second[c])
            tlow[2 * c + b] = both[:, 0:128]

    spread = dot(tlow[...].reshape(48, 128), halves[...])
    own_g = jnp.sum(jnp.where(keep48[...] > 0.0, spread, 0.0), axis=0, keepdims=True)
    gsend[...] = own_g
    round_b = [send(gsend, grecv.at[k], d) for k, d in enumerate(column)]

    low = iota((8, 128), 0) < 4
    for side, (at, extra) in enumerate(((0, 0), (0, 8))):
        total = jnp.zeros((8, 128), F32)
        for f in range(4):
            for x in range(4):
                s = 4 * f + x
                moved = pltpu.roll(km[f, 2 + x, :, 0:128], (8 * s + extra) % 128, 1)
                total = jnp.where(slot8 == s, moved, total)
        mpack[side] = jnp.where(low, total, pltpu.roll(total, 4, 0))
    round_c = []
    mid_x = {-1: slice(8, 12), 0: slice(4, 8), 1: slice(0, 4)}
    mid_row = {-1: slice(4, 8), 0: slice(0, 4), 1: slice(12, 16)}
    block = km.at[:, 2:6, 0:4, 0:128]
    for d in flat:
        round_c.append(send(block, wd.at[:, mid_x[d[0]], mid_row[d[1]], 0:128], d))
    for d in tilted:
        side = 0 if d[2] < 0 else 1
        round_c.append(send(mpack.at[side], mrecv.at[side, 1 - d[0], 1 - d[1]], d))
    for f in range(4):
        wd[f, 4:8, 0:4, 0:128] = km[f, 2:6, 0:4, 0:128]
        wd[f, :, 8:12, 0:128] = jnp.zeros((12, 4, 128), F32)
    for copy in loads[2:]:
        copy.wait()
    for copy in round_b:
        copy.wait_recv()
    g = own_g + jnp.sum(grecv[...], axis=0)
    g = jnp.broadcast_to(g, (8, g.shape[1]))
    w = lax.dot_general(
        g, rows[...], (((1,), (1,)), ((), ())), precision=HIGH, preferred_element_type=F32
    )
    wsend[...] = w[0:1, :]
    round_d = [send(wsend, wrecv.at[1 - d[0], 1 - d[1]], d) for d in flat]

    for copy in round_c:
        copy.wait_recv()
    for ox in range(3):
        near_y = [jnp.where(low, mrecv[side, ox, 1], mrecv[side, ox, 2]) for side in range(2)]
        far_y = [mrecv[side, ox, 0] for side in range(2)]
        for f in range(4):
            for x in range(4):
                s = 4 * f + x
                wd[f, 4 * ox + x, 0:8, 128:256] = rim(near_y[0], near_y[1], s)
                wd[f, 4 * ox + x, 8:16, 128:256] = rim(far_y[0], far_y[1], s)
    row16 = iota((16, 256), 0)
    lane16 = iota((16, 256), 1)
    y_at = gy * 4 + jnp.where(row16 < 8, row16, row16 - 16)
    z_at = gz * 128 + jnp.where(lane16 < 192, lane16, lane16 - 256)
    inside = (y_at >= 0) & (y_at < 4 * ng[1]) & (z_at >= 0) & (z_at < 128 * ng[2])
    inside = inside & ((row16 < 8) | (row16 >= 12)) & ((lane16 < 136) | (lane16 >= 248))
    inside = jnp.where(inside, 1, 0)

    @pl.loop(0, 12, unroll=4)
    def _(x):
        x_at = gx * 4 + x - 4
        x_in = jnp.where((x_at >= 0) & (x_at < 4 * ng[0]), 1, 0)
        wd[3, x] = jnp.where(inside * x_in > 0, wd[3, x], 0.0)

    @pl.loop(1, 11, unroll=2)
    def _(x):
        own, inverse = centre_terms(wd[3, x - 1], wd[3, x], wd[3, x + 1])
        cenw[x] = own
        dinvw[x] = inverse
        for c in range(3):
            m_b[c, x] = inverse * wd[c, x]

    col = iota((16, 128), 1)
    blk = col // 24
    keep = (col < 72) & ((col % 24) // 2 == iota((16, 128), 0))
    keep = keep & ((blk != 0) | (gz > 0)) & ((blk != 2) | (gz < ng[2] - 1))
    for copy in round_d:
        copy.wait_recv()
    picked = []
    for ox in range(3):
        for oy in range(3):
            x_at, y_at = gx + (ox - 1), gy + (oy - 1)
            known = (x_at >= 0) & (x_at < ng[0]) & (y_at >= 0) & (y_at < ng[1])
            line = wsend[...] if (ox, oy) == (1, 1) else wrecv[ox, oy]
            line = jnp.broadcast_to(line * jnp.where(known, 1.0, 0.0), (16, 128))
            picked.append(jnp.where(keep, line, 0.0))
    blocks = dot(jnp.concatenate(picked, axis=0), sel[...])

    row_in_8 = iota((8, 256), 0)
    for ox in range(3):
        values = [blocks[16 * (3 * ox + oy) : 16 * (3 * ox + oy) + 16] for oy in range(3)]
        for xb in range(2):
            for c in range(3):
                r = 4 * c + 2 * xb

                def line(oy, k, r=r, values=values):
                    return jnp.broadcast_to(values[oy][r + k : r + k + 1, :], (8, 256))

                upper_tile = jnp.where(
                    row_in_8 < 4,
                    jnp.where(row_in_8 < 2, line(1, 0), line(1, 1)),
                    jnp.where(row_in_8 < 6, line(2, 0), line(2, 1)),
                )
                lower_tile = jnp.where(row_in_8 < 6, line(0, 0), line(0, 1))
                for x in (4 * ox + 2 * xb, 4 * ox + 2 * xb + 1):
                    if 1 <= x < 11:
                        m_b[c, x, 0:8] += upper_tile
                        m_b[c, x, 8:16] += lower_tile

    @pl.loop(0, 4)
    def _(k):
        x = 2 * k + 2
        images = operate(lambda c, k: m_b[c, k], lambda k: wd[3, k], lambda k: cenw[k], x, 2)
        for i, image in enumerate(images):
            for c in range(3):
                value = m_b[c, x + i] + dinvw[x + i] * (wd[c, x + i] - image[c])
                u8[c, x + i - 2] = jnp.where(row_in_8 < 6, value[0:8], value[8:16])

    fine_u = dot(u8[...].reshape(192, 256), rz_mat[...], (((1,), (1,)), ((), ()))).reshape(3, 8, 8, 384)
    for t in range(3):
        piece = fine_u[:, :, :, 128 * t : 128 * t + 128]
        ysum[0:3, :, t, pl.ds(0, 8, stride=2), :] = piece
        ysum[0:3, :, t, pl.ds(1, 8, stride=2), :] = piece

    @pl.loop(1, 15, unroll=2)
    def _(x):
        k = x // 2
        for c in range(3):
            for t in range(3):
                lanes = slice(128 * t, 128 * t + 128)
                s_a[c, x, :, lanes] = s_b[c, x, :, lanes] + ysum[c, k, t]

    sweep(s_a, s_b, 2, 14, 3)
    sweep(s_b, s_a, 3, 13, 5)

    def last(k, sums):
        new = list(sums)
        for i, image in enumerate(fine(s_a)(2 * k + 4, 2)):
            x = 2 * k + i
            for c in range(3):
                p = s_a[c, x + 4, 0:8, 0:256]
                ap = image[c][0:8, 0:256]
                d = pdir[c, x]
                q = pimg[c, x]
                p_out[c, x] = p
                ap_out[c, x] = ap
                terms = (res[c, x + 4, 0:8, 0:256] * p, p * ap, p * q + d * ap, d * q)
                new = [a + b for a, b in zip(new, terms)]
        return tuple(new)

    zero = jnp.zeros((8, 256), F32)
    stores = [
        pltpu.make_async_copy(p_out, held_hbm.at[0], lsem.at[0]),
        pltpu.make_async_copy(ap_out, held_hbm.at[1], lsem.at[1]),
    ]
    sums = lax.fori_loop(0, 4, last, (zero, zero, zero, zero))
    group = iota((1, 128), 1) // 32
    mine = jnp.zeros((1, 128), F32)
    for i, value in enumerate(sums):
        value = jnp.sum(value[:, 0:128] + value[:, 128:256], axis=0, keepdims=True)
        value = value + pltpu.roll(value, 64, 1)
        value = value + pltpu.roll(value, 32, 1)
        mine = jnp.where(group == i, value, mine)

    pending = list(started)
    for peers, out, into in ((layer, dsend, drecv), (column, esend, erecv)):
        out[...] = mine
        copies = [send(out, into.at[k], d) for k, d in enumerate(peers)]
        if peers is layer:
            for copy in stores:
                copy.start()
        else:
            for copy in stores:
                copy.wait()
        for copy in pending:
            copy.wait_send()
        pending = copies
        for copy in copies:
            copy.wait_recv()
        mine = mine + jnp.sum(into[...], axis=0)
    inner_rz, pp, cross, qq = (
        jnp.sum(jnp.where(group == i, mine, 0.0), axis=1, keepdims=True) for i in range(4)
    )
    beta = inner_rz / prev_rz[0]
    alpha = inner_rz / (pp + beta * (cross + beta * qq))
    ab_out[...] = jnp.broadcast_to(jnp.where(group < 2, alpha, beta), (8, 128))
    last_store = pltpu.make_async_copy(ab_out, held_hbm.at[2, 0, 0, :, 0:128], lsem.at[2])
    last_store.start()
    last_store.wait()
    for copy in pending:
        copy.wait_send()


def finish(pdir, pimg, sol, res, held_hbm, *refs):
    targets, held, ab, made, sems, outs = refs[0:4], refs[4], refs[5], refs[6:10], refs[10], refs[11]
    ab_load = pltpu.make_async_copy(held_hbm.at[2, 0, 0, :, 0:128], ab, sems.at[3, 0])
    ab_load.start()
    loads = [[pltpu.make_async_copy(held_hbm.at[i, c], held.at[i, c], sems.at[c, i]) for i in range(2)] for c in range(3)]
    for part in loads:
        for copy in part:
            copy.start()
    p, ap = held.at[0], held.at[1]
    new_sol, new_res, new_dir, new_img = made
    ab_load.wait()
    alpha = jnp.broadcast_to(ab[0:1, 0:1], (8, 256))
    beta = jnp.broadcast_to(ab[0:1, 64:65], (8, 256))
    stores = []
    for c in range(3):
        for copy in loads[c]:
            copy.wait()
        for x in range(p.shape[1]):
            direction = p[c, x] + beta * pdir[c, x]
            image = ap[c, x] + beta * pimg[c, x]
            new_dir[c, x] = direction
            new_img[c, x] = image
            new_sol[c, x] = sol[c, x] + alpha * direction
            new_res[c, x] = res[c, x] - alpha * image
        for i, (src, dst) in enumerate(zip(made, targets)):
            copy = pltpu.make_async_copy(src.at[c], dst.at[c], outs.at[c, i])
            copy.start()
            stores.append(copy)
    for copy in stores:
        copy.wait()


def solution(mesh):
    ng = tuple(mesh.shape[a] for a in AXES)

    def on_device(sol, res, pdir, pimg, prev_rz, dens, table, inverse):
        def vm(*shape):
            return pltpu.VMEM(shape, F32)

        kc = inverse.shape[3]
        n_layer, n_col = ng[0] * ng[1] - 1, ng[2] - 1
        copies = 16 + 18 + 26 + 8 + n_layer + 2 * n_col
        scratch = [
            pltpu.VMEM((8, 8, 256), jnp.int32),
            vm(3, 16, 16, 384),
            vm(18, 24, 384),
            vm(16, 16, 384), vm(16, 16, 384), vm(16, 16, 384),
            vm(3, 16, 16, 384), vm(3, 16, 16, 384),
            vm(3, 8, 8, 256), vm(3, 8, 8, 256),
            vm(2, 2, 8, 128), vm(2, 3, 3, 2, 8, 128),
            vm(4, 8, 3, 16, 128),
            vm(4, 8, 8, 256), vm(8, 8, 256), vm(8, 8, 256), vm(3, 8, 8, 256),
            vm(6, 8, 128),
            vm(2, 8, 128), vm(2, 3, 3, 8, 128),
            vm(4, 12, 16, 256), vm(12, 16, 256), vm(12, 16, 256),
            vm(3, 12, 16, 256), vm(8, 128), vm(3, 8, 8, 256),
            pltpu.VMEM((384, 256), jnp.bfloat16), pltpu.VMEM((128, 256), jnp.bfloat16),
            pltpu.VMEM((128, kc), jnp.bfloat16), vm(48, kc),
            vm(1, kc), vm(n_col, 1, kc), vm(128, kc),
            vm(1, 128), vm(3, 3, 1, 128),
            vm(1, 128), vm(n_layer, 1, 128), vm(1, 128), vm(n_col, 1, 128),
            vm(3, 8, 8, 256), vm(3, 8, 8, 256), vm(8, 128),
            pltpu.SMEM(table.shape, F32), pltpu.SMEM((1,), F32),
            pltpu.SemaphoreType.DMA((9,)),
            pltpu.SemaphoreType.DMA((copies,)),
            pltpu.SemaphoreType.DMA((copies,)),
        ]
        in_hbm = pl.BlockSpec(memory_space=pltpu.HBM)
        in_vmem = pl.BlockSpec(memory_space=pltpu.VMEM)
        field = jax.ShapeDtypeStruct(res.shape, F32)
        held = pl.pallas_call(
            functools.partial(kernel, ng),
            name="cg_step",
            out_shape=jax.ShapeDtypeStruct((HELD,) + res.shape, F32),
            in_specs=[in_hbm] * 7,
            out_specs=in_hbm,
            scratch_shapes=scratch,
            compiler_params=pltpu.CompilerParams(
                collective_id=0, has_side_effects=True, vmem_limit_bytes=56 << 20
            ),
        )(res, pdir, pimg, dens, inverse, table, prev_rz.reshape(1))
        return pl.pallas_call(
            finish,
            name="cg_finish",
            out_shape=(field,) * 4,
            in_specs=[in_vmem] * 4 + [in_hbm],
            out_specs=(in_hbm,) * 4,
            scratch_shapes=[vm(2, *res.shape), vm(8, 128)] + [vm(*res.shape)] * 4
            + [pltpu.SemaphoreType.DMA((4, 2)), pltpu.SemaphoreType.DMA((3, 4))],
            compiler_params=pltpu.CompilerParams(vmem_limit_bytes=16 << 20),
        )(pdir, pimg, sol, res, held)

    split = P(None, *AXES)
    return jax.shard_map(
        on_device,
        mesh=mesh,
        in_specs=(split, split, split, split, P(), P(*AXES), P(), P("gx", "gy", None, None)),
        out_specs=(split, split, split, split),
        check_vma=False,
    )
```
